32 devices in a mesh: groups: 2 (over y), section: 4 (over z), head: 4 (over x, core).
Axes of the slice: x: 2, y: 2, z: 4, core: 2. Of those that a mesh axis runs over, the one named last changes fastest.
Arguments:
- queries: bfloat16 [1024, 2048], P(('groups', 'section'), 'head'), parts along dimension 0, may hold values from -16 to 16
- token_key_rows: bfloat16 [1024, 1024], P(('groups', 'section'), 'head'), parts along dimension 0, may hold values from -16 to 16
- token_value_rows: bfloat16 [1024, 1024], P(('groups', 'section'), 'head'), parts along dimension 0, may hold values from -6 to 6
- residual: bfloat16 [1024, 5376], P(('groups', 'section', 'head')), parts along dimension 0, may hold values from -6 to 6
- prefix: int32 [8], P('groups'), parts along dimension 0, may hold values from 0 to 128, as said below
- out_weight: bfloat16 [2048, 5376], P('head', 'section'), may hold values from -1 to 1
- post_gain: float32 [5376], replicated, may hold values from 0.25 to 1.75
Outputs:
- layer_out: bfloat16 [1024, 5376], P(('groups', 'section', 'head')), parts along dimension 0
The draws below stay inside these ranges and needn't reach their ends.
There are 2 independent parts, one for each index of `groups`. The reference program is written for one: setup_inputs(seed, part) draws one part's arguments, and reference() takes and returns one part's arrays. A program takes and returns all parts, laid end to end along the dimension named above; an argument that names none is the same for every part. Nothing has to cross between parts.
Inputs may be any that keep to these rules, and one draw needn't show every extreme that they name: `prefix`: some section at index 1 or higher has the most, 128.
All inputs are finite; a program needn't handle non-finite values.
Results may differ from the reference program's by a relative error of at most 0.012.
Values may be sent and summed in bfloat16 or wider, within the bound.
A program may use at most 64 MiB of HBM per device.

```python
import jax
import jax.numpy as jnp
from jax import lax

D = 5376
HEAD_SIZE = 128
QUERY_HEADS = 16
KEY_VALUE_HEADS = 8
SECTION_ROWS = 128
SEQUENCE_TOKENS = 512
REACH = 1
N_SECTION = 4
N_HEAD = 4


def drawn_pair(key):
    starting_key = jax.random.fold_in(key, 71)
    query_tile_block = jnp.clip(jax.random.normal(jax.random.fold_in(starting_key, 8), (SEQUENCE_TOKENS, QUERY_HEADS * HEAD_SIZE), jnp.float32), -6.0, 6.0)
    key_tile_block = jnp.clip(jax.random.normal(jax.random.fold_in(starting_key, 9), (SEQUENCE_TOKENS, KEY_VALUE_HEADS * HEAD_SIZE), jnp.float32), -6.0, 6.0)
    return (query_tile_block, key_tile_block)


def draw_queries(key, part):
    return drawn_pair(key)[0].astype(jnp.bfloat16)


def draw_token_key_rows(key, part):
    return drawn_pair(key)[1].astype(jnp.bfloat16)


def draw_prefix(key, part):
    section_count = SEQUENCE_TOKENS // SECTION_ROWS
    longest = REACH * SECTION_ROWS
    lengths = jax.random.randint(jax.random.fold_in(key, 301), (section_count,), 0, longest + 1)
    chosen = jax.random.randint(jax.random.fold_in(key, 302), (), REACH, section_count)
    marked = jnp.arange(section_count, dtype=jnp.int32) == chosen
    return jnp.where(marked, longest, lengths).astype(jnp.int32)


def draw_out_weight(key, part):
    fan_in = QUERY_HEADS * HEAD_SIZE
    entries = jnp.clip(jax.random.normal(jax.random.fold_in(key, 403), (fan_in, D), jnp.float32), -6.0, 6.0)
    return (entries * fan_in ** (-0.5)).astype(jnp.bfloat16)


def level_of(key, extent, shards, least, largest):
    gain = 1.0
    for axis_at, blocks in shards:
        heights = jax.random.uniform(jax.random.fold_in(jax.random.fold_in(key, 6), axis_at), (blocks,), jnp.float32, least / len(shards), largest / len(shards))
        gain = gain * jnp.repeat(jnp.exp(heights), extent[axis_at] // blocks).reshape((-1,) + (1,) * (len(extent) - 1 - axis_at))
    return gain


def scatter_about(stream_key, shape, deviation, most, cuts=(), kind=jnp.bfloat16):
    drawn = deviation * jax.random.normal(stream_key, shape, jnp.float32)
    if cuts:
        drawn = drawn * level_of(stream_key, shape, cuts, -0.22, 0.18)
    return jnp.clip(drawn, -most, most).astype(kind)


def setup_inputs(seed: int = 0, part: int = 0) -> dict:
    streams_of = jax.random.split(jax.random.key(seed), 8)
    own_keys = jax.random.split(jax.random.fold_in(streams_of[7], part), 8)
    queries = draw_queries(jax.random.fold_in(jax.random.fold_in(streams_of[7], part), 71), part)
    token_key_rows = draw_token_key_rows(jax.random.fold_in(jax.random.fold_in(streams_of[7], part), 71), part)
    token_value_rows = scatter_about(own_keys[2], (SEQUENCE_TOKENS, KEY_VALUE_HEADS * HEAD_SIZE), 1.0, 6.0, ((0, 4), (1, 4)))
    residual = scatter_about(own_keys[3], (SEQUENCE_TOKENS, D), 1.0, 6.0, ((0, 16),))
    prefix = draw_prefix(jax.random.fold_in(jax.random.fold_in(streams_of[7], part), 71), part)
    out_weight = draw_out_weight(jax.random.fold_in(streams_of[7], 71), part)
    post_gain = jnp.clip(1.0 + 0.15 * jax.random.normal(streams_of[6], (D,), jnp.float32), 0.25, 1.75)
    return dict(queries=queries, token_key_rows=token_key_rows, token_value_rows=token_value_rows, residual=residual, prefix=prefix, out_weight=out_weight, post_gain=post_gain)


score_scale = 168.0 ** (-0.5)
norm_eps = 1e-06

def reference(queries, token_key_rows, token_value_rows, residual, prefix, out_weight, post_gain):
    reachable_blocks = 3 * N_SECTION // 8
    prefix_window_rows = (reachable_blocks + 1) * SECTION_ROWS
    group_width = QUERY_HEADS // KEY_VALUE_HEADS
    head_columns = QUERY_HEADS * HEAD_SIZE // N_HEAD
    extended_keys = jnp.concatenate([jnp.zeros((reachable_blocks * SECTION_ROWS, KEY_VALUE_HEADS * HEAD_SIZE), token_key_rows.dtype), token_key_rows], axis=0)
    extended_values = jnp.concatenate([jnp.zeros((reachable_blocks * SECTION_ROWS, KEY_VALUE_HEADS * HEAD_SIZE), token_value_rows.dtype), token_value_rows], axis=0)

    def one_section(section_at):
        first_row = (section_at * SECTION_ROWS).astype(jnp.int32)
        query_tile_block = lax.dynamic_slice_in_dim(queries, first_row, SECTION_ROWS, 0).astype(jnp.float32)
        query_tile_block = query_tile_block.reshape(SECTION_ROWS, KEY_VALUE_HEADS, group_width, HEAD_SIZE)
        key_tile_block = lax.dynamic_slice_in_dim(extended_keys, first_row, prefix_window_rows, 0).astype(jnp.float32)
        key_tile_block = key_tile_block.reshape(prefix_window_rows, KEY_VALUE_HEADS, HEAD_SIZE)
        value_tile_block = lax.dynamic_slice_in_dim(extended_values, first_row, prefix_window_rows, 0).astype(jnp.float32)
        value_tile_block = value_tile_block.reshape(prefix_window_rows, KEY_VALUE_HEADS, HEAD_SIZE)
        query_pos = first_row + jnp.arange(SECTION_ROWS, dtype=jnp.int32)
        key_pos = first_row - reachable_blocks * SECTION_ROWS + jnp.arange(prefix_window_rows, dtype=jnp.int32)
        seen_tokens = jnp.minimum(first_row, prefix[section_at])
        lower_pos = first_row - seen_tokens
        visible = (key_pos[None, :] <= query_pos[:, None]) & (key_pos[None, :] >= lower_pos)
        scores = jnp.einsum('qkgd,pkd->kgqp', query_tile_block, key_tile_block) * score_scale
        masked = jnp.where(visible, scores, -jnp.inf)
        row_max = lax.optimization_barrier(jnp.max(masked, axis=-1))
        weights = jnp.where(visible, jnp.exp(masked - row_max[..., None]), 0.0)
        denominator = lax.optimization_barrier(jnp.sum(weights, axis=-1))
        weights_low = lax.optimization_barrier(weights.astype(jnp.bfloat16))
        combined = jnp.einsum('kgqp,pkd->qkgd', weights_low.astype(jnp.float32), value_tile_block)
        attention = combined / jnp.transpose(denominator, (2, 0, 1))[..., None]
        attention = attention.reshape(SECTION_ROWS, QUERY_HEADS * HEAD_SIZE).astype(jnp.bfloat16)
        summed = jnp.zeros((SECTION_ROWS, D), jnp.float32)
        for head_at in range(N_HEAD):
            column_block = attention[:, head_at * head_columns:(head_at + 1) * head_columns]
            weight_rows = out_weight[head_at * head_columns:(head_at + 1) * head_columns]
            partial_value = jnp.dot(column_block, weight_rows, preferred_element_type=jnp.float32)
            partial_value = lax.optimization_barrier(partial_value.astype(jnp.bfloat16))
            summed = summed + partial_value.astype(jnp.float32)
        residual_block = lax.dynamic_slice_in_dim(residual, first_row, SECTION_ROWS, 0).astype(jnp.float32)
        mean_square = lax.optimization_barrier(jnp.mean(summed * summed, axis=-1, keepdims=True))
        normed = summed * lax.rsqrt(mean_square + norm_eps) * post_gain.astype(jnp.float32)[None, :]
        return (residual_block + normed).astype(jnp.bfloat16)
    section_outputs = lax.map(one_section, jnp.arange(N_SECTION, dtype=jnp.int32))
    return section_outputs.reshape(SEQUENCE_TOKENS, D)
```

```python
import functools

import jax
import jax.numpy as jnp
from jax import lax
from jax.experimental import pallas as pl
from jax.experimental.pallas import tpu as pltpu
from jax.sharding import PartitionSpec as P

HEAD_SIZE = 128


score_scale = 168.0 ** (-0.5)
floor_value = -1e30
norm_eps = 1e-06
LANES = 128
CHUNKS = 2
VMEM_LIMIT = (60 * 1024 - 720) * 1024
MESH = pl.DeviceIdType.MESH


COST = {"S": 0.03, "R": 0.03, "M": 0.55, "P": 0.06, "F": 0.08, "N": 0.15}
BIAS = {"S": -2.0, "R": 0.0, "F": 0.3, "P": 0.0, "M": -0.2, "N": 1.0}
TURN = "SRFPMN"


@functools.lru_cache(None)
def schedules(n, chunks):
    piece, slab, hop, base = 1.42, 1.96 / chunks, 0.75, 1.0
    first = [5.0] + [7.05 + 0.75 * s for s in range(1, n)]
    busy, crossing, clock = {(0, 1): 6.0}, [0.0] * n, list(first)
    order, tasks, got = [[] for _ in range(n)], [{} for _ in range(n)], [{} for _ in range(n)]

    def along(source, target, length, t):
        step = 1 if target > source else -1
        for at in range(source, target, step):
            t = max(t, busy.get((at, at + step), 0.0))
            busy[at, at + step] = t + length
            t += hop
        return t + length + base

    def reduced(s, b, c):
        pair = [got[s].get((side, b, c)) for side in ("far", "near")]
        if None not in pair:
            tasks[s]["F", b, c] = max(pair)

    for s in range(n):
        for j in range(2):
            tasks[s]["M", s, j] = first[s]
            for step in (-1, 1):
                if 0 <= s + step < n:
                    tasks[s]["S", step, j] = first[s] if s else busy[0, 1]

    while any(tasks):
        _, s, task = min(
            (
                (max(clock[s], t) + BIAS[task[0]], TURN.index(task[0]), task[2], task[1]),
                s,
                task,
            )
            for s in range(n)
            for task, t in tasks[s].items()
        )
        begin = max(clock[s], tasks[s].pop(task))
        kind, b, j = task
        order[s].append(task)
        end = clock[s] = begin + COST[kind]
        if kind == "S":
            tasks[s + b]["R", s, j] = along(s, s + b, piece, end)
        elif kind == "R":
            tasks[s]["M", b, j] = end
            target = s + 1 if b < s else s - 1
            if 0 <= target < n:
                tasks[target]["R", b, j] = along(s, target, piece, end)
        elif kind == "M":
            for c in range(chunks):
                t = begin + COST[kind] * (c + 1) / chunks + 0.6
                if j == 0:
                    tasks[s]["P", b, c] = t
                else:
                    got[s]["near", b, c] = t
                    reduced(s, b, c)
        elif kind == "P":
            crossing[s] = max(end, crossing[s]) + slab
            got[s]["far", b, j] = crossing[s] + 2.1
            reduced(s, b, j)
        elif kind == "F":
            tasks[b]["N", s, j] = end if b == s else along(s, b, slab, end)
    return order


def fused_kernel(
    n,
    heads,
    chunks,
    prefix_hbm,
    q_hbm,
    k_hbm,
    v_hbm,
    w_hbm,
    res_hbm,
    gain_hbm,
    out_ref,
    prefix_ref,
    q_v,
    k_v,
    v_v,
    k_prev,
    v_prev,
    w_v,
    w_t,
    res_v,
    gain_v,
    gain_w,
    attn,
    pair_send,
    pair_recv,
    mine,
    far_send,
    far_recv,
    done_send,
    done_recv,
    scaled,
    load_sem,
    kv_send_sem,
    kv_recv_sem,
    attn_send_sem,
    attn_recv_sem,
    pair_send_sem,
    pair_recv_sem,
    far_send_sem,
    far_recv_sem,
    done_send_sem,
    done_recv_sem,
):
    me = lax.axis_index("section")
    h = lax.axis_index("head")
    rows = q_hbm.shape[0]
    own_rows = rows // heads
    core = lax.rem(h, 2)
    partner = h + 1 - 2 * core
    far = lax.rem(h + 2, heads)
    group_rows = 2 * own_rows
    starts = [
        pl.multiple_of(lax.rem(h // 2 + 1 + j, 2) * group_rows, group_rows) for j in range(2)
    ]
    key_heads = k_hbm.shape[1] // HEAD_SIZE
    group_width = q_hbm.shape[1] // k_hbm.shape[1]
    width = w_hbm.shape[0]
    edges = [LANES * round(width * c / (chunks * LANES)) for c in range(chunks)] + [width]
    spans = [slice(edges[c], edges[c + 1]) for c in range(chunks)]

    def remote(source, target, send_sem, recv_sem, where):
        return pltpu.make_async_remote_copy(
            src_ref=source,
            dst_ref=target,
            send_sem=send_sem,
            recv_sem=recv_sem,
            device_id=where,
            device_id_type=MESH,
        )

    loads = [
        pltpu.make_async_copy(source, target, load_sem.at[i])
        for i, (source, target) in enumerate(
            (
                (prefix_hbm, prefix_ref),
                (q_hbm, q_v),
                (k_hbm, k_v),
                (v_hbm, v_v),
                (w_hbm, w_v),
                (res_hbm, res_v),
                (gain_hbm, gain_v),
            )
        )
    ]
    has_below, has_above = me > 0, me + 1 < n
    barrier = pltpu.get_barrier_semaphore()
    for there, step in ((has_below, -1), (has_above, 1)):

        @pl.when(there)
        def _(step=step):
            pl.semaphore_signal(
                barrier, inc=1, device_id={"section": me + step}, device_id_type=MESH
            )

    for other in (partner, far):
        pl.semaphore_signal(barrier, inc=1, device_id={"head": other}, device_id_type=MESH)
    for load in loads:
        load.start()
    for load in loads[:4]:
        load.wait()
    pl.semaphore_wait(
        barrier, 2 + jnp.where(has_below, 1, 0) + jnp.where(has_above, 1, 0)
    )

    def head_span(at):
        return slice(at * HEAD_SIZE, (at + 1) * HEAD_SIZE)

    def kv_copies(kh):
        above = {"section": lax.rem(me + 1, n)}
        span = head_span(kh)
        return [
            remote(
                source.at[:, span],
                target.at[:, span],
                kv_send_sem.at[i],
                kv_recv_sem.at[kh],
                above,
            )
            for i, (source, target) in enumerate(((k_v, k_prev), (v_v, v_prev)))
        ]

    @pl.when(has_above)
    def _():
        for kh in range(key_heads):
            for copy in kv_copies(kh):
                copy.start()

    @pl.when(me == 0)
    def _():
        k_prev[...] = jnp.zeros_like(k_prev)
        v_prev[...] = jnp.zeros_like(v_prev)

    seen = jnp.minimum(me * rows, prefix_ref[me])
    wide = group_width * rows
    q_row = lax.rem(lax.broadcasted_iota(jnp.int32, (wide, rows), 0), rows)
    k_col = lax.broadcasted_iota(jnp.int32, (wide, rows), 1)
    own_seen = k_col <= q_row
    prev_seen = k_col >= rows - seen

    def head_columns(ref, at):
        return ref[:, head_span(at)]

    def scores_of(query, key):
        return (
            lax.dot_general(
                query, key, (((1,), (1,)), ((), ())), preferred_element_type=jnp.float32
            )
            * score_scale
        )

    queries = [
        jnp.concatenate(
            [head_columns(q_v, kh * group_width + g) for g in range(group_width)], axis=0
        )
        for kh in range(key_heads)
    ]
    own_parts = []
    for kh in range(key_heads):
        own = jnp.where(own_seen, scores_of(queries[kh], head_columns(k_v, kh)), floor_value)
        own_top = jnp.max(own, axis=-1, keepdims=True)
        own_probs = jnp.where(own_seen, jnp.exp(own - own_top), 0.0)
        own_total = jnp.sum(own_probs, axis=-1, keepdims=True)
        own_combined = jnp.dot(
            own_probs.astype(jnp.bfloat16),
            head_columns(v_v, kh),
            preferred_element_type=jnp.float32,
        )
        own_parts.append((own_top, own_total, own_combined))

    for load in loads[4:]:
        load.wait()
    w_t[...] = w_v[...].T
    gain_w[...] = jnp.broadcast_to(gain_v[...][None, :], gain_w.shape)

    for kh in range(key_heads):

        @pl.when(has_below)
        def _(kh=kh):
            remote(
                k_prev, k_prev, kv_send_sem.at[0], kv_recv_sem.at[kh], {"section": me - 1}
            ).wait_recv()

        own_top, own_total, own_combined = own_parts[kh]
        prev = jnp.where(
            prev_seen, scores_of(queries[kh], head_columns(k_prev, kh)), floor_value
        )
        top = jnp.maximum(own_top, jnp.max(prev, axis=-1, keepdims=True))
        prev_probs = jnp.where(prev_seen, jnp.exp(prev - top), 0.0)
        carry = jnp.exp(own_top - top)
        total = carry * own_total + jnp.sum(prev_probs, axis=-1, keepdims=True)
        combined = carry * own_combined + jnp.dot(
            prev_probs.astype(jnp.bfloat16),
            head_columns(v_prev, kh),
            preferred_element_type=jnp.float32,
        )
        result = (combined / total).astype(jnp.bfloat16)
        for g in range(group_width):
            attn[me, :, head_span(kh * group_width + g)] = result[g * rows : (g + 1) * rows]

    def attn_copy(slot, block, j, target):
        here = attn.at[block, pl.ds(starts[j], group_rows)]
        return remote(
            here,
            here,
            attn_send_sem.at[slot],
            attn_recv_sem.at[block, j],
            {"section": target},
        )

    def pair_copy(b, j, c):
        return remote(
            pair_send.at[b, j, :, spans[c]],
            pair_recv.at[b, j, :, spans[c]],
            pair_send_sem,
            pair_recv_sem.at[b, c if j == 0 else chunks],
            {"head": partner},
        )

    def far_copy(b, c):
        return remote(
            far_send.at[b, :, spans[c]],
            far_recv.at[b, :, spans[c]],
            far_send_sem,
            far_recv_sem.at[b, c],
            {"head": far},
        )

    def done_copy(source, b, c):
        return remote(
            done_send.at[b, :, spans[c]],
            done_recv.at[source, :, spans[c]],
            done_send_sem,
            done_recv_sem.at[source],
            {"section": b},
        )

    def wide_of(block):
        return block.astype(jnp.float32)

    def run(s):
        reached = {s - 1, s + 1} & set(range(n))
        onward = {b: (s + 1 if b < s else s - 1) for b in range(n) if b != s}
        onward = {b: t for b, t in onward.items() if 0 <= t < n}
        squares = []
        started, passed, paired = [], [], []

        def whole(ref, send_sem, recv_sem):
            return remote(ref, ref, send_sem, recv_sem, {"head": partner})


        def wait_kv_sent():
            for i, source in enumerate((k_v, v_v)):
                remote(
                    source, source, kv_send_sem.at[i], kv_recv_sem.at[0], {"section": s + 1}
                ).wait_send()

        def send_own(step, j):
            if s == 0 and not started:
                wait_kv_sent()
            started.append(j)
            attn_copy(0, s, j, s + step).start()

        def relay(b, j):
            attn_copy(1, b, j, s).wait_recv()
            if b in onward:
                passed.append(j)
                attn_copy(1, b, j, onward[b]).start()

        def multiply(b, j):
            left = jnp.concatenate(
                [
                    attn[b, pl.ds(pl.multiple_of(starts[j] + side * own_rows, own_rows), own_rows)]
                    for side in (1 - core, core)
                ],
                axis=0,
            )
            for c in range(chunks):
                product = jnp.dot(left, w_t[:, spans[c]], preferred_element_type=jnp.float32)
                pair_send[b, j, :, spans[c]] = product[:own_rows].astype(jnp.bfloat16)
                mine[b, j, :, spans[c]] = product[own_rows:]
                pair_copy(b, j, c).start()

        def add_pair(b, c):
            span = spans[c]
            pair_copy(b, 0, c).wait_recv()
            far_send[b, :, span] = (
                mine[b, 0, :, span] + wide_of(pair_recv[b, 0, :, span])
            ).astype(jnp.bfloat16)
            far_copy(b, c).start()

        def add_far(b, c):
            span = spans[c]
            if b not in paired:
                paired.append(b)
                whole(pair_send.at[b, 1], pair_send_sem, pair_recv_sem.at[b, chunks]).wait_recv()
            far_copy(b, c).wait_recv()
            value = (
                mine[b, 1, :, span]
                + wide_of(pair_recv[b, 1, :, span])
                + wide_of(far_recv[b, :, span])
            ).astype(jnp.bfloat16)
            if b == s:
                done_recv[s, :, span] = value
            else:
                done_send[b, :, span] = value
                done_copy(s, b, c).start()

        def gather(b, c):
            if c + 1 < chunks:
                return
            if b != s:
                whole(done_recv.at[b], done_send_sem, done_recv_sem.at[b]).wait_recv()
            value = wide_of(done_recv[b])
            squares.append(jnp.sum(value * value, axis=-1, keepdims=True))
            columns = slice(b * width, (b + 1) * width)
            scaled[:, columns] = value * gain_w[:, columns]

        actions = {
            "S": send_own,
            "R": relay,
            "M": multiply,
            "P": add_pair,
            "F": add_far,
            "N": gather,
        }
        for kind, b, j in schedules(n, chunks)[s]:
            actions[kind](b, j)
        scale = lax.rsqrt(sum(squares) / (n * width) + norm_eps)
        out_ref[...] = (wide_of(res_v[...]) + scaled[...] * scale).astype(out_ref.dtype)

        if s != 0 and s + 1 < n:
            wait_kv_sent()
        for slot, sent in enumerate((started, passed)):
            if sent:
                half = attn.at[0 : len(sent) // 2]
                whole(half, attn_send_sem.at[slot], attn_recv_sem.at[s, 0]).wait_send()
        whole(pair_send, pair_send_sem, pair_recv_sem.at[s, 0]).wait_send()
        whole(far_send, far_send_sem, far_recv_sem.at[s, 0]).wait_send()
        whole(done_send.at[: n - 1], done_send_sem, done_recv_sem.at[s]).wait_send()

    for s in range(n):

        @pl.when(me == s)
        def _(s=s):
            run(s)


def fused_local(
    n, heads, queries, token_key_rows, token_value_rows, residual, prefix, out_weight, post_gain
):
    rows = queries.shape[0]
    own_rows = rows // heads
    width = out_weight.shape[1]
    key_heads = token_key_rows.shape[1] // HEAD_SIZE
    low = jnp.bfloat16
    stays = pl.BlockSpec(memory_space=pltpu.HBM)
    vector = pl.BlockSpec(memory_space=pltpu.VMEM)
    dma = pltpu.SemaphoreType.DMA
    weights = out_weight.T
    part = (n, own_rows, width)
    return pl.pallas_call(
        functools.partial(fused_kernel, n, heads, CHUNKS),
        out_shape=pltpu.VMEM(residual.shape, low),
        in_specs=[stays] * 7,
        out_specs=vector,
        scratch_shapes=[
            pltpu.SMEM(prefix.shape, jnp.int32),
            pltpu.VMEM(queries.shape, low),
            pltpu.VMEM(token_key_rows.shape, low),
            pltpu.VMEM(token_value_rows.shape, low),
            pltpu.VMEM(token_key_rows.shape, low),
            pltpu.VMEM(token_value_rows.shape, low),
            pltpu.VMEM(weights.shape, low),
            pltpu.VMEM(out_weight.shape, low),
            pltpu.VMEM(residual.shape, low),
            pltpu.VMEM(post_gain.shape, jnp.float32),
            pltpu.VMEM((own_rows,) + post_gain.shape, jnp.float32),
            pltpu.VMEM((n, rows, queries.shape[1]), low),
            pltpu.VMEM((n, 2, own_rows, width), low),
            pltpu.VMEM((n, 2, own_rows, width), low),
            pltpu.VMEM((n, 2, own_rows, width), jnp.float32),
            pltpu.VMEM(part, low),
            pltpu.VMEM(part, low),
            pltpu.VMEM(part, low),
            pltpu.VMEM(part, low),
            pltpu.VMEM(residual.shape, jnp.float32),
            dma((7,)),
            dma((2,)),
            dma((key_heads,)),
            dma((2,)),
            dma((n, 2)),
            dma,
            dma((n, CHUNKS + 1)),
            dma,
            dma((n, CHUNKS)),
            dma,
            dma((n,)),
        ],
        compiler_params=pltpu.CompilerParams(
            collective_id=0, has_side_effects=True, vmem_limit_bytes=VMEM_LIMIT
        ),
    )(prefix, queries, token_key_rows, token_value_rows, weights, residual, post_gain)


def shifted(value, axis, steps):
    count = lax.axis_size(axis)
    leading, last = (max(0, -steps), min(count, count - steps))
    return lax.ppermute(value, axis, [(source, source + steps) for source in range(leading, last)])


def empty_state(row_count, key_heads, group_width):
    running_max = jnp.full((key_heads, group_width, row_count), floor_value, jnp.float32)
    running_sum = jnp.zeros((key_heads, group_width, row_count), jnp.float32)
    weighted = jnp.zeros((row_count, key_heads, group_width, HEAD_SIZE), jnp.float32)
    return (running_max, running_sum, weighted)


def attend(
    status, query_tile_block, query_pos, lower_pos, key_tile_block, value_tile_block, key_pos
):
    running_max, running_sum, weighted = status
    row_count = query_tile_block.shape[0]
    key_heads = key_tile_block.shape[1] // HEAD_SIZE
    group_width = query_tile_block.shape[1] // (key_heads * HEAD_SIZE)
    query_four = query_tile_block.reshape(row_count, key_heads, group_width, HEAD_SIZE)
    key_three = key_tile_block.reshape(key_tile_block.shape[0], key_heads, HEAD_SIZE)
    value_three = value_tile_block.reshape(value_tile_block.shape[0], key_heads, HEAD_SIZE)
    scores = (
        jnp.einsum("qkgd,pkd->kgqp", query_four, key_three, preferred_element_type=jnp.float32)
        * score_scale
    )
    visible = (key_pos[None, :] <= query_pos[:, None]) & (key_pos[None, :] >= lower_pos)
    masked = jnp.where(visible, scores, floor_value)
    new_max = jnp.maximum(running_max, jnp.max(masked, axis=-1))
    carry_scale = jnp.exp(running_max - new_max)
    weights = jnp.where(visible, jnp.exp(masked - new_max[..., None]), 0.0)
    running_sum = carry_scale * running_sum + jnp.sum(weights, axis=-1)
    product = jnp.einsum(
        "kgqp,pkd->qkgd",
        weights.astype(jnp.bfloat16),
        value_three,
        preferred_element_type=jnp.float32,
    )
    weighted = jnp.transpose(carry_scale, (2, 0, 1))[..., None] * weighted + product
    return (new_max, running_sum, weighted)


def local(queries, token_key_rows, token_value_rows, residual, prefix, out_weight, post_gain):
    row_count = queries.shape[0]
    key_heads = token_key_rows.shape[1] // HEAD_SIZE
    group_width = queries.shape[1] // (key_heads * HEAD_SIZE)
    section_total = lax.axis_size("section")
    section_index = lax.axis_index("section")
    reachable_blocks = 3 * section_total // 8
    base_rows = jnp.arange(row_count, dtype=jnp.int32)
    own_pos = section_index * row_count + base_rows
    seen_tokens = jnp.minimum(section_index * row_count, prefix[section_index])
    lower_pos = section_index * row_count - seen_tokens
    block_count = (seen_tokens + row_count - 1) // row_count
    blank = empty_state(row_count, key_heads, group_width)
    states = attend(blank, queries, own_pos, lower_pos, token_key_rows, token_value_rows, own_pos)

    def process(distance, key_tile_block, value_tile_block, mine):
        key_pos = (section_index - distance) * row_count + base_rows
        use_mine = distance <= block_count
        return lax.cond(
            use_mine,
            lambda current: attend(
                current, queries, own_pos, lower_pos, key_tile_block, value_tile_block, key_pos
            ),
            lambda current: current,
            mine,
        )

    held_keys = token_key_rows[None]
    held_values = token_value_rows[None]
    stride = 1
    while stride <= reachable_blocks:
        amount_moved = min(stride, reachable_blocks + 1 - stride)
        moved_keys, moved_values = shifted(
            (held_keys[:amount_moved], held_values[:amount_moved]), "section", stride
        )
        held_keys = jnp.concatenate([held_keys, moved_keys], axis=0)
        held_values = jnp.concatenate([held_values, moved_values], axis=0)
        stride = stride * 2

    def visit_block(distance, inner):
        key_tile_block = lax.dynamic_index_in_dim(held_keys, distance, 0, keepdims=False)
        value_tile_block = lax.dynamic_index_in_dim(held_values, distance, 0, keepdims=False)
        return process(distance, key_tile_block, value_tile_block, inner)

    states = lax.fori_loop(1, reachable_blocks + 1, visit_block, states)
    attention = states[2] / jnp.transpose(states[1], (2, 0, 1))[..., None]
    attention = attention.reshape(row_count, key_heads * group_width * HEAD_SIZE).astype(
        jnp.bfloat16
    )
    partial_out = jnp.dot(
        attention,
        lax.all_gather(out_weight, "section", axis=1, tiled=True),
        preferred_element_type=jnp.float32,
    )
    summed = lax.psum_scatter(
        partial_out.astype(jnp.bfloat16), "head", scatter_dimension=0, tiled=True
    ).astype(jnp.float32)
    mean_square = jnp.mean(summed * summed, axis=-1, keepdims=True)
    normed = summed * lax.rsqrt(mean_square + norm_eps) * post_gain[None, :]
    return (residual.astype(jnp.float32) + normed).astype(jnp.bfloat16)


def solution(mesh):
    placed = (
        P(("groups", "section"), "head"),
        P(("groups", "section"), "head"),
        P(("groups", "section"), "head"),
        P(("groups", "section", "head"), None),
        P("groups"),
        P("head", "section"),
        P(),
    )
    n, heads = mesh.shape["section"], mesh.shape["head"]
    body = local
    if 3 * n // 8 == 1 and heads == 4:
        body = functools.partial(fused_local, n, heads)
    return jax.shard_map(
        body,
        mesh=mesh,
        in_specs=placed,
        out_specs=P(("groups", "section", "head"), None),
        check_vma=False,
    )
```

```python
import functools

import jax
import jax.numpy as jnp
from jax import lax
from jax.experimental import pallas as pl
from jax.experimental.pallas import tpu as pltpu
from jax.sharding import PartitionSpec as P

HEAD_SIZE = 128


score_scale = 168.0 ** (-0.5)
floor_value = -1e30
norm_eps = 1e-06
LANES = 128
CHUNKS = 2
VMEM_LIMIT = (60 * 1024 - 720) * 1024
MESH = pl.DeviceIdType.MESH


ORDERS = {
    4: (
        (
            "S10", "S11", "S12", "S13", "M00", "M01", "P00", "P01", "R10", "M10", "R11", "P10",
            "P11", "M11", "R20", "M20", "R21", "P20", "P21", "M21", "F10", "F11", "R30", "R31",
            "M30", "P30", "P31", "F20", "R32", "F21", "R33", "M31", "F30", "F31", "F00", "F01",
            "N00", "N01", "N10", "N11", "N20", "N21", "N30", "N31",
        ),
        (
            "S-10", "S10", "S-11", "S11", "M10", "M11", "P10", "P11", "R00", "R01", "M00", "R02",
            "R03", "P00", "P01", "R20", "M20", "R21", "P20", "P21", "M01", "M21", "R30", "R31",
            "M30", "R32", "P30", "P31", "R33", "M31", "F00", "F01", "F20", "F21", "F30", "F31",
            "F10", "F11", "N10", "N11", "N00", "N01", "N20", "N21", "N30", "N31",
        ),
        (
            "S-10", "S10", "S-11", "S11", "M20", "M21", "P20", "P21", "R30", "R31", "R10", "M10",
            "R32", "R00", "P10", "P11", "R01", "R33", "M00", "P00", "P01", "R02", "R03", "R11",
            "M11", "M01", "M30", "P30", "P31", "F10", "F11", "M31", "F00", "F01", "F30", "F31",
            "F20", "F21", "N20", "N21", "N30", "N31", "N10", "N11", "N00", "N01",
        ),
        (
            "S-10", "S-11", "S-12", "S-13", "M30", "M31", "P30", "P31", "R20", "M20", "P20",
            "P21", "R21", "M21", "R00", "R01", "M00", "P00", "P01", "R10", "M10", "R02", "R03",
            "M01", "P10", "P11", "F20", "F21", "F00", "F01", "R11", "M11", "F10", "F11", "F30",
            "F31", "N30", "N31", "N20", "N21", "N10", "N11", "N00", "N01",
        ),
    ),
}


def fused_kernel(
    n,
    heads,
    chunks,
    prefix_hbm,
    q_hbm,
    k_hbm,
    v_hbm,
    w_hbm,
    res_hbm,
    gain_hbm,
    out_ref,
    prefix_ref,
    q_v,
    k_v,
    v_v,
    k_prev,
    v_prev,
    w_v,
    w_t,
    res_v,
    gain_v,
    gain_w,
    attn,
    pair_send,
    pair_recv,
    mine,
    far_send,
    far_recv,
    done_send,
    done_recv,
    scaled,
    load_sem,
    kv_send_sem,
    kv_recv_sem,
    attn_send_sem,
    attn_recv_sem,
    pair_send_sem,
    pair_recv_sem,
    far_send_sem,
    far_recv_sem,
    done_send_sem,
    done_recv_sem,
):
    me = lax.axis_index("section")
    h = lax.axis_index("head")
    rows = q_hbm.shape[0]
    own_rows = rows // heads
    core = lax.rem(h, 2)
    partner = h + 1 - 2 * core
    far = lax.rem(h + 2, heads)
    group_rows = 2 * own_rows
    starts = [
        pl.multiple_of(lax.rem(h // 2 + 1 + j, 2) * group_rows, group_rows) for j in range(2)
    ]
    key_heads = k_hbm.shape[1] // HEAD_SIZE
    group_width = q_hbm.shape[1] // k_hbm.shape[1]
    width = w_hbm.shape[0]
    edges = [LANES * round(width * c / (chunks * LANES)) for c in range(chunks)] + [width]
    spans = [slice(edges[c], edges[c + 1]) for c in range(chunks)]

    def remote(source, target, send_sem, recv_sem, where):
        return pltpu.make_async_remote_copy(
            src_ref=source,
            dst_ref=target,
            send_sem=send_sem,
            recv_sem=recv_sem,
            device_id=where,
            device_id_type=MESH,
        )

    loads = [
        pltpu.make_async_copy(source, target, load_sem.at[i])
        for i, (source, target) in enumerate(
            (
                (prefix_hbm, prefix_ref),
                (q_hbm, q_v),
                (k_hbm, k_v),
                (v_hbm, v_v),
                (w_hbm, w_v),
                (res_hbm, res_v),
                (gain_hbm, gain_v),
            )
        )
    ]
    has_below, has_above = me > 0, me + 1 < n
    barrier = pltpu.get_barrier_semaphore()
    for there, step in ((has_below, -1), (has_above, 1)):

        @pl.when(there)
        def _(step=step):
            pl.semaphore_signal(
                barrier, inc=1, device_id={"section": me + step}, device_id_type=MESH
            )

    for other in (partner, far):
        pl.semaphore_signal(barrier, inc=1, device_id={"head": other}, device_id_type=MESH)
    for load in loads:
        load.start()
    for load in loads[:4]:
        load.wait()
    pl.semaphore_wait(
        barrier, 2 + jnp.where(has_below, 1, 0) + jnp.where(has_above, 1, 0)
    )

    def head_span(at):
        return slice(at * HEAD_SIZE, (at + 1) * HEAD_SIZE)

    def kv_copies(kh):
        above = {"section": lax.rem(me + 1, n)}
        span = head_span(kh)
        return [
            remote(
                source.at[:, span],
                target.at[:, span],
                kv_send_sem.at[i],
                kv_recv_sem.at[kh],
                above,
            )
            for i, (source, target) in enumerate(((k_v, k_prev), (v_v, v_prev)))
        ]

    @pl.when(has_above)
    def _():
        for kh in range(key_heads):
            for copy in kv_copies(kh):
                copy.start()

    @pl.when(me == 0)
    def _():
        k_prev[...] = jnp.zeros_like(k_prev)
        v_prev[...] = jnp.zeros_like(v_prev)

    seen = jnp.minimum(me * rows, prefix_ref[me])
    wide = group_width * rows
    q_row = lax.rem(lax.broadcasted_iota(jnp.int32, (wide, rows), 0), rows)
    k_col = lax.broadcasted_iota(jnp.int32, (wide, rows), 1)
    own_seen = k_col <= q_row
    prev_seen = k_col >= rows - seen

    def head_columns(ref, at):
        return ref[:, head_span(at)]

    def scores_of(query, key):
        return (
            lax.dot_general(
                query, key, (((1,), (1,)), ((), ())), preferred_element_type=jnp.float32
            )
            * score_scale
        )

    queries = [
        jnp.concatenate(
            [head_columns(q_v, kh * group_width + g) for g in range(group_width)], axis=0
        )
        for kh in range(key_heads)
    ]
    own_parts = []
    for kh in range(key_heads):
        own = jnp.where(own_seen, scores_of(queries[kh], head_columns(k_v, kh)), floor_value)
        own_top = jnp.max(own, axis=-1, keepdims=True)
        own_probs = jnp.where(own_seen, jnp.exp(own - own_top), 0.0)
        own_total = jnp.sum(own_probs, axis=-1, keepdims=True)
        own_combined = jnp.dot(
            own_probs.astype(jnp.bfloat16),
            head_columns(v_v, kh),
            preferred_element_type=jnp.float32,
        )
        own_parts.append((own_top, own_total, own_combined))

    for load in loads[4:]:
        load.wait()
    w_t[...] = w_v[...].T
    gain_w[...] = jnp.broadcast_to(gain_v[...][None, :], gain_w.shape)

    for kh in range(key_heads):

        @pl.when(has_below)
        def _(kh=kh):
            remote(
                k_prev, k_prev, kv_send_sem.at[0], kv_recv_sem.at[kh], {"section": me - 1}
            ).wait_recv()

        own_top, own_total, own_combined = own_parts[kh]
        prev = jnp.where(
            prev_seen, scores_of(queries[kh], head_columns(k_prev, kh)), floor_value
        )
        top = jnp.maximum(own_top, jnp.max(prev, axis=-1, keepdims=True))
        prev_probs = jnp.where(prev_seen, jnp.exp(prev - top), 0.0)
        carry = jnp.exp(own_top - top)
        total = carry * own_total + jnp.sum(prev_probs, axis=-1, keepdims=True)
        combined = carry * own_combined + jnp.dot(
            prev_probs.astype(jnp.bfloat16),
            head_columns(v_prev, kh),
            preferred_element_type=jnp.float32,
        )
        result = (combined / total).astype(jnp.bfloat16)
        for g in range(group_width):
            attn[me, :, head_span(kh * group_width + g)] = result[g * rows : (g + 1) * rows]

    def parts_of(block):
        return 4 if block in (0, n - 1) else 2

    def attn_copy(slot, block, j, target):
        count = 2 * group_rows // parts_of(block)
        half, at = divmod(j * count, group_rows)
        here = attn.at[block, pl.ds(pl.multiple_of(starts[half] + at, count), count)]
        return remote(
            here,
            here,
            attn_send_sem.at[slot],
            attn_recv_sem.at[sum(parts_of(b) for b in range(block)) + j],
            {"section": target},
        )

    def pair_copy(b, j, c):
        return remote(
            pair_send.at[b, j, :, spans[c]],
            pair_recv.at[b, j, :, spans[c]],
            pair_send_sem,
            pair_recv_sem.at[b, c if j == 0 else chunks],
            {"head": partner},
        )

    def far_copy(b, c):
        return remote(
            far_send.at[b, :, spans[c]],
            far_recv.at[b, :, spans[c]],
            far_send_sem,
            far_recv_sem.at[b, c],
            {"head": far},
        )

    def done_copy(source, b, c):
        return remote(
            done_send.at[b, :, spans[c]],
            done_recv.at[source, :, spans[c]],
            done_send_sem,
            done_recv_sem.at[source],
            {"section": b},
        )

    def wide_of(block):
        return block.astype(jnp.float32)

    def run(s):
        reached = {s - 1, s + 1} & set(range(n))
        onward = {b: (s + 1 if b < s else s - 1) for b in range(n) if b != s}
        onward = {b: t for b, t in onward.items() if 0 <= t < n}
        squares = []
        started, passed, paired = [], [], []

        def whole(ref, send_sem, recv_sem):
            return remote(ref, ref, send_sem, recv_sem, {"head": partner})


        def wait_kv_sent():
            for i, source in enumerate((k_v, v_v)):
                remote(
                    source, source, kv_send_sem.at[i], kv_recv_sem.at[0], {"section": s + 1}
                ).wait_send()

        def send_own(step, j):
            if s == 0 and not started:
                wait_kv_sent()
            started.append(parts_of(s))
            attn_copy(0, s, j, s + step).start()

        def relay(b, j):
            attn_copy(1, b, j, s).wait_recv()
            if b in onward:
                passed.append(parts_of(b))
                attn_copy(1, b, j, onward[b]).start()

        def multiply(b, j):
            left = jnp.concatenate(
                [
                    attn[b, pl.ds(pl.multiple_of(starts[j] + side * own_rows, own_rows), own_rows)]
                    for side in (1 - core, core)
                ],
                axis=0,
            )
            for c in range(chunks):
                product = jnp.dot(left, w_t[:, spans[c]], preferred_element_type=jnp.float32)
                pair_send[b, j, :, spans[c]] = product[:own_rows].astype(jnp.bfloat16)
                mine[b, j, :, spans[c]] = product[own_rows:]
                pair_copy(b, j, c).start()

        def add_pair(b, c):
            span = spans[c]
            pair_copy(b, 0, c).wait_recv()
            far_send[b, :, span] = (
                mine[b, 0, :, span] + wide_of(pair_recv[b, 0, :, span])
            ).astype(jnp.bfloat16)
            far_copy(b, c).start()

        def add_far(b, c):
            span = spans[c]
            if b not in paired:
                paired.append(b)
                whole(pair_send.at[b, 1], pair_send_sem, pair_recv_sem.at[b, chunks]).wait_recv()
            far_copy(b, c).wait_recv()
            value = (
                mine[b, 1, :, span]
                + wide_of(pair_recv[b, 1, :, span])
                + wide_of(far_recv[b, :, span])
            ).astype(jnp.bfloat16)
            if b == s:
                done_recv[s, :, span] = value
            else:
                done_send[b, :, span] = value
                done_copy(s, b, c).start()

        def gather(b, c):
            if c + 1 < chunks:
                return
            if b != s:
                whole(done_recv.at[b], done_send_sem, done_recv_sem.at[b]).wait_recv()
            value = wide_of(done_recv[b])
            squares.append(jnp.sum(value * value, axis=-1, keepdims=True))
            columns = slice(b * width, (b + 1) * width)
            scaled[:, columns] = value * gain_w[:, columns]

        actions = {
            "S": send_own,
            "R": relay,
            "M": multiply,
            "P": add_pair,
            "F": add_far,
            "N": gather,
        }
        for step in ORDERS[n][s]:
            kind, b, j = step[0], int(step[1:-1]), int(step[-1])
            actions[kind](b, j)
        scale = lax.rsqrt(sum(squares) / (n * width) + norm_eps)
        out_ref[...] = (wide_of(res_v[...]) + scaled[...] * scale).astype(out_ref.dtype)

        if s != 0 and s + 1 < n:
            wait_kv_sent()
        for slot, sent in enumerate((started, passed)):
            if sent:
                half = attn.at[0 : round(sum(1 / parts for parts in sent))]
                whole(half, attn_send_sem.at[slot], attn_recv_sem.at[0]).wait_send()
        whole(pair_send, pair_send_sem, pair_recv_sem.at[s, 0]).wait_send()
        whole(far_send, far_send_sem, far_recv_sem.at[s, 0]).wait_send()
        whole(done_send.at[: n - 1], done_send_sem, done_recv_sem.at[s]).wait_send()

    for s in range(n):

        @pl.when(me == s)
        def _(s=s):
            run(s)


def fused_local(
    n, heads, queries, token_key_rows, token_value_rows, residual, prefix, out_weight, post_gain
):
    rows = queries.shape[0]
    own_rows = rows // heads
    width = out_weight.shape[1]
    key_heads = token_key_rows.shape[1] // HEAD_SIZE
    low = jnp.bfloat16
    stays = pl.BlockSpec(memory_space=pltpu.HBM)
    vector = pl.BlockSpec(memory_space=pltpu.VMEM)
    dma = pltpu.SemaphoreType.DMA
    weights = out_weight.T
    part = (n, own_rows, width)
    return pl.pallas_call(
        functools.partial(fused_kernel, n, heads, CHUNKS),
        out_shape=pltpu.VMEM(residual.shape, low),
        in_specs=[stays] * 7,
        out_specs=vector,
        scratch_shapes=[
            pltpu.SMEM(prefix.shape, jnp.int32),
            pltpu.VMEM(queries.shape, low),
            pltpu.VMEM(token_key_rows.shape, low),
            pltpu.VMEM(token_value_rows.shape, low),
            pltpu.VMEM(token_key_rows.shape, low),
            pltpu.VMEM(token_value_rows.shape, low),
            pltpu.VMEM(weights.shape, low),
            pltpu.VMEM(out_weight.shape, low),
            pltpu.VMEM(residual.shape, low),
            pltpu.VMEM(post_gain.shape, jnp.float32),
            pltpu.VMEM((own_rows,) + post_gain.shape, jnp.float32),
            pltpu.VMEM((n, rows, queries.shape[1]), low),
            pltpu.VMEM((n, 2, own_rows, width), low),
            pltpu.VMEM((n, 2, own_rows, width), low),
            pltpu.VMEM((n, 2, own_rows, width), jnp.float32),
            pltpu.VMEM(part, low),
            pltpu.VMEM(part, low),
            pltpu.VMEM(part, low),
            pltpu.VMEM(part, low),
            pltpu.VMEM(residual.shape, jnp.float32),
            dma((7,)),
            dma((2,)),
            dma((key_heads,)),
            dma((2,)),
            dma((2 * n + 4,)),
            dma,
            dma((n, CHUNKS + 1)),
            dma,
            dma((n, CHUNKS)),
            dma,
            dma((n,)),
        ],
        compiler_params=pltpu.CompilerParams(
            collective_id=0, has_side_effects=True, vmem_limit_bytes=VMEM_LIMIT
        ),
    )(prefix, queries, token_key_rows, token_value_rows, weights, residual, post_gain)


def shifted(value, axis, steps):
    count = lax.axis_size(axis)
    leading, last = (max(0, -steps), min(count, count - steps))
    return lax.ppermute(value, axis, [(source, source + steps) for source in range(leading, last)])


def empty_state(row_count, key_heads, group_width):
    running_max = jnp.full((key_heads, group_width, row_count), floor_value, jnp.float32)
    running_sum = jnp.zeros((key_heads, group_width, row_count), jnp.float32)
    weighted = jnp.zeros((row_count, key_heads, group_width, HEAD_SIZE), jnp.float32)
    return (running_max, running_sum, weighted)


def attend(
    status, query_tile_block, query_pos, lower_pos, key_tile_block, value_tile_block, key_pos
):
    running_max, running_sum, weighted = status
    row_count = query_tile_block.shape[0]
    key_heads = key_tile_block.shape[1] // HEAD_SIZE
    group_width = query_tile_block.shape[1] // (key_heads * HEAD_SIZE)
    query_four = query_tile_block.reshape(row_count, key_heads, group_width, HEAD_SIZE)
    key_three = key_tile_block.reshape(key_tile_block.shape[0], key_heads, HEAD_SIZE)
    value_three = value_tile_block.reshape(value_tile_block.shape[0], key_heads, HEAD_SIZE)
    scores = (
        jnp.einsum("qkgd,pkd->kgqp", query_four, key_three, preferred_element_type=jnp.float32)
        * score_scale
    )
    visible = (key_pos[None, :] <= query_pos[:, None]) & (key_pos[None, :] >= lower_pos)
    masked = jnp.where(visible, scores, floor_value)
    new_max = jnp.maximum(running_max, jnp.max(masked, axis=-1))
    carry_scale = jnp.exp(running_max - new_max)
    weights = jnp.where(visible, jnp.exp(masked - new_max[..., None]), 0.0)
    running_sum = carry_scale * running_sum + jnp.sum(weights, axis=-1)
    product = jnp.einsum(
        "kgqp,pkd->qkgd",
        weights.astype(jnp.bfloat16),
        value_three,
        preferred_element_type=jnp.float32,
    )
    weighted = jnp.transpose(carry_scale, (2, 0, 1))[..., None] * weighted + product
    return (new_max, running_sum, weighted)


def local(queries, token_key_rows, token_value_rows, residual, prefix, out_weight, post_gain):
    row_count = queries.shape[0]
    key_heads = token_key_rows.shape[1] // HEAD_SIZE
    group_width = queries.shape[1] // (key_heads * HEAD_SIZE)
    section_total = lax.axis_size("section")
    section_index = lax.axis_index("section")
    reachable_blocks = 3 * section_total // 8
    base_rows = jnp.arange(row_count, dtype=jnp.int32)
    own_pos = section_index * row_count + base_rows
    seen_tokens = jnp.minimum(section_index * row_count, prefix[section_index])
    lower_pos = section_index * row_count - seen_tokens
    block_count = (seen_tokens + row_count - 1) // row_count
    blank = empty_state(row_count, key_heads, group_width)
    states = attend(blank, queries, own_pos, lower_pos, token_key_rows, token_value_rows, own_pos)

    def process(distance, key_tile_block, value_tile_block, mine):
        key_pos = (section_index - distance) * row_count + base_rows
        use_mine = distance <= block_count
        return lax.cond(
            use_mine,
            lambda current: attend(
                current, queries, own_pos, lower_pos, key_tile_block, value_tile_block, key_pos
            ),
            lambda current: current,
            mine,
        )

    held_keys = token_key_rows[None]
    held_values = token_value_rows[None]
    stride = 1
    while stride <= reachable_blocks:
        amount_moved = min(stride, reachable_blocks + 1 - stride)
        moved_keys, moved_values = shifted(
            (held_keys[:amount_moved], held_values[:amount_moved]), "section", stride
        )
        held_keys = jnp.concatenate([held_keys, moved_keys], axis=0)
        held_values = jnp.concatenate([held_values, moved_values], axis=0)
        stride = stride * 2

    def visit_block(distance, inner):
        key_tile_block = lax.dynamic_index_in_dim(held_keys, distance, 0, keepdims=False)
        value_tile_block = lax.dynamic_index_in_dim(held_values, distance, 0, keepdims=False)
        return process(distance, key_tile_block, value_tile_block, inner)

    states = lax.fori_loop(1, reachable_blocks + 1, visit_block, states)
    attention = states[2] / jnp.transpose(states[1], (2, 0, 1))[..., None]
    attention = attention.reshape(row_count, key_heads * group_width * HEAD_SIZE).astype(
        jnp.bfloat16
    )
    partial_out = jnp.dot(
        attention,
        lax.all_gather(out_weight, "section", axis=1, tiled=True),
        preferred_element_type=jnp.float32,
    )
    summed = lax.psum_scatter(
        partial_out.astype(jnp.bfloat16), "head", scatter_dimension=0, tiled=True
    ).astype(jnp.float32)
    mean_square = jnp.mean(summed * summed, axis=-1, keepdims=True)
    normed = summed * lax.rsqrt(mean_square + norm_eps) * post_gain[None, :]
    return (residual.astype(jnp.float32) + normed).astype(jnp.bfloat16)


def solution(mesh):
    placed = (
        P(("groups", "section"), "head"),
        P(("groups", "section"), "head"),
        P(("groups", "section"), "head"),
        P(("groups", "section", "head"), None),
        P("groups"),
        P("head", "section"),
        P(),
    )
    n, heads = mesh.shape["section"], mesh.shape["head"]
    body = local
    if n in ORDERS and 3 * n // 8 == 1 and heads == 4:
        body = functools.partial(fused_local, n, heads)
    return jax.shard_map(
        body,
        mesh=mesh,
        in_specs=placed,
        out_specs=P(("groups", "section", "head"), None),
        check_vma=False,
    )
```

```python
import functools

import jax
import jax.numpy as jnp
from jax import lax
from jax.experimental import pallas as pl
from jax.experimental.pallas import tpu as pltpu
from jax.sharding import PartitionSpec as P

HEAD_SIZE = 128


score_scale = 168.0 ** (-0.5)
floor_value = -1e30
norm_eps = 1e-06
LANES = 128
FARTHER = 1
VMEM_LIMIT = (60 * 1024 - 720) * 1024
MESH = pl.DeviceIdType.MESH


ORDERS = {
    4: (
        (
            "M00", "M01", "S10", "S11", "S12", "S13", "P00", "R10", "M10", "R11", "P10", "P11",
            "M11", "R20", "M20", "R21", "P20", "P21", "M21", "F10", "F11", "R30", "R31", "M30",
            "P30", "P31", "F20", "R32", "F21", "R33", "M31", "F30", "F31", "F00", "N00", "N10",
            "N20", "N30",
        ),
        (
            "S-10", "S10", "S-11", "S11", "M10", "M11", "P10", "R00", "R01", "M00", "R02", "R03",
            "P00", "P01", "R20", "M20", "R21", "P20", "P21", "M01", "M21", "R30", "R31", "M30",
            "R32", "P30", "P31", "R33", "M31", "F00", "F01", "F20", "F21", "F30", "F31", "F10",
            "N10", "N00", "N20", "N30",
        ),
        (
            "S-10", "S10", "S-11", "S11", "M20", "M21", "P20", "R10", "M10", "R30", "R31", "P10",
            "P11", "R00", "R32", "R01", "M00", "R33", "P00", "P01", "R02", "R03", "R11", "M11",
            "M01", "F10", "F11", "M30", "P30", "P31", "M31", "F00", "F01", "F30", "F31", "F20",
            "N20", "N30", "N10", "N00",
        ),
        (
            "S-10", "S-11", "S-12", "S-13", "M30", "M31", "P30", "R20", "M20", "P20", "P21",
            "R21", "M21", "R00", "R01", "M00", "P00", "P01", "R10", "M10", "R02", "R03", "M01",
            "P10", "P11", "F20", "F21", "F00", "F01", "R11", "M11", "F10", "F11", "F30", "N30",
            "N20", "N10", "N00",
        ),
    ),
}


def pieces_of(s, b, n):
    return 1 if abs(b - s) < FARTHER else 2


def fused_kernel(
    n,
    heads,
    prefix_hbm,
    q_hbm,
    k_hbm,
    v_hbm,
    w_hbm,
    res_hbm,
    gain_hbm,
    out_ref,
    prefix_ref,
    q_v,
    k_v,
    v_v,
    k_prev,
    v_prev,
    w_v,
    w_t,
    res_v,
    gain_v,
    gain_w,
    attn,
    pair_send,
    pair_recv,
    mine,
    far_send,
    far_recv,
    done_send,
    done_recv,
    scaled,
    load_sem,
    kv_send_sem,
    kv_recv_sem,
    attn_send_sem,
    attn_recv_sem,
    pair_send_sem,
    pair_recv_sem,
    far_send_sem,
    far_recv_sem,
    done_send_sem,
    done_recv_sem,
    cleared,
):
    me = lax.axis_index("section")
    h = lax.axis_index("head")
    rows = q_hbm.shape[0]
    own_rows = rows // heads
    core = lax.rem(h, 2)
    partner = h + 1 - 2 * core
    far = lax.rem(h + 2, heads)
    group_rows = 2 * own_rows
    starts = [
        pl.multiple_of(lax.rem(h // 2 + 1 + j, 2) * group_rows, group_rows) for j in range(2)
    ]
    key_heads = k_hbm.shape[1] // HEAD_SIZE
    group_width = q_hbm.shape[1] // k_hbm.shape[1]
    width = w_hbm.shape[0]

    def cut(count):
        edges = [LANES * round(width * c / (count * LANES)) for c in range(count)] + [width]
        return [slice(a, b) for a, b in zip(edges, edges[1:])]

    def remote(source, target, send_sem, recv_sem, where):
        return pltpu.make_async_remote_copy(
            src_ref=source,
            dst_ref=target,
            send_sem=send_sem,
            recv_sem=recv_sem,
            device_id=where,
            device_id_type=MESH,
        )

    loads = [
        pltpu.make_async_copy(source, target, load_sem.at[i])
        for i, (source, target) in enumerate(
            (
                (prefix_hbm, prefix_ref),
                (q_hbm, q_v),
                (k_hbm, k_v),
                (v_hbm, v_v),
                (w_hbm, w_v),
                (res_hbm, res_v),
                (gain_hbm, gain_v),
            )
        )
    ]
    has_below, has_above = me > 0, me + 1 < n
    barrier = pltpu.get_barrier_semaphore()
    for there, step in ((has_below, -1), (has_above, 1)):

        @pl.when(there)
        def _(step=step):
            pl.semaphore_signal(
                barrier, inc=1, device_id={"section": me + step}, device_id_type=MESH
            )

    for other in (partner, far):
        pl.semaphore_signal(barrier, inc=1, device_id={"head": other}, device_id_type=MESH)
    for load in loads:
        load.start()
    for load in loads[:4]:
        load.wait()
    pl.semaphore_wait(
        barrier, 2 + jnp.where(has_below, 1, 0) + jnp.where(has_above, 1, 0)
    )

    def head_span(at):
        return slice(at * HEAD_SIZE, (at + 1) * HEAD_SIZE)

    def kv_copies():
        return [
            remote(
                source,
                target,
                kv_send_sem.at[i],
                kv_recv_sem.at[i],
                {"section": lax.rem(me + 1, n)},
            )
            for i, (source, target) in enumerate(((k_v, k_prev), (v_v, v_prev)))
        ]

    @pl.when(has_above)
    def _():
        for copy in kv_copies():
            copy.start()

    @pl.when(me == 0)
    def _():
        k_prev[...] = jnp.zeros_like(k_prev)
        v_prev[...] = jnp.zeros_like(v_prev)

    seen = jnp.minimum(me * rows, prefix_ref[me])
    wide = group_width * rows
    q_row = lax.rem(lax.broadcasted_iota(jnp.int32, (wide, rows), 0), rows)
    k_col = lax.broadcasted_iota(jnp.int32, (wide, rows), 1)
    own_seen = k_col <= q_row
    prev_seen = k_col >= rows - seen

    def head_columns(ref, at):
        return ref[:, head_span(at)]

    def scores_of(query, key):
        return (
            lax.dot_general(
                query, key, (((1,), (1,)), ((), ())), preferred_element_type=jnp.float32
            )
            * score_scale
        )

    queries = [
        jnp.concatenate(
            [head_columns(q_v, kh * group_width + g) for g in range(group_width)], axis=0
        )
        for kh in range(key_heads)
    ]
    own_parts = []
    for kh in range(key_heads):
        own = jnp.where(own_seen, scores_of(queries[kh], head_columns(k_v, kh)), floor_value)
        own_top = jnp.max(own, axis=-1, keepdims=True)
        own_probs = jnp.where(own_seen, jnp.exp(own - own_top), 0.0)
        own_total = jnp.sum(own_probs, axis=-1, keepdims=True)
        own_combined = jnp.dot(
            own_probs.astype(jnp.bfloat16),
            head_columns(v_v, kh),
            preferred_element_type=jnp.float32,
        )
        own_parts.append((own_top, own_total, own_combined))

    for load in loads[4:]:
        load.wait()
    w_t[...] = w_v[...].T
    gain_w[...] = jnp.broadcast_to(gain_v[...][None, :], gain_w.shape)

    @pl.when(has_below)
    def _():
        kv_copies()[0].wait_recv()

    joined = []
    for kh in range(key_heads):
        own_top, own_total, own_combined = own_parts[kh]
        prev = jnp.where(
            prev_seen, scores_of(queries[kh], head_columns(k_prev, kh)), floor_value
        )
        top = jnp.maximum(own_top, jnp.max(prev, axis=-1, keepdims=True))
        prev_probs = jnp.where(prev_seen, jnp.exp(prev - top), 0.0)
        carry = jnp.exp(own_top - top)
        inverse = 1.0 / (carry * own_total + jnp.sum(prev_probs, axis=-1, keepdims=True))
        joined.append((prev_probs.astype(jnp.bfloat16), carry * own_combined, inverse))

    @pl.when(has_below)
    def _():
        kv_copies()[1].wait_recv()

    for kh in range(key_heads):
        prev_probs, own_combined, inverse = joined[kh]
        combined = own_combined + jnp.dot(
            prev_probs, head_columns(v_prev, kh), preferred_element_type=jnp.float32
        )
        result = (combined * inverse).astype(jnp.bfloat16)
        for g in range(group_width):
            attn[me, :, head_span(kh * group_width + g)] = result[g * rows : (g + 1) * rows]

    def parts_of(block):
        return 4 if block in (0, n - 1) else 2

    def attn_copy(slot, block, j, target):
        count = 2 * group_rows // parts_of(block)
        half, at = divmod(j * count, group_rows)
        here = attn.at[block, pl.ds(pl.multiple_of(starts[half] + at, count), count)]
        return remote(
            here,
            here,
            attn_send_sem.at[slot],
            attn_recv_sem.at[sum(parts_of(b) for b in range(block)) + j],
            {"section": target},
        )

    def wide_of(block):
        return block.astype(jnp.float32)

    def run(s):
        onward = {b: (s + 1 if b < s else s - 1) for b in range(n) if b != s}
        onward = {b: t for b, t in onward.items() if 0 <= t < n}
        squares = []
        started, passed, paired = [], [], []

        spans = [cut(pieces_of(s, b, n)) for b in range(n)]
        bases = [sum(map(len, spans[:b])) for b in range(n)]

        def pair_copy(b, j, c):
            span = spans[b][c]
            at = bases[b] + c if j == 0 else bases[-1] + len(spans[-1]) + b
            return remote(
                pair_send.at[b, j, :, span],
                pair_recv.at[b, j, :, span],
                pair_send_sem,
                pair_recv_sem.at[at],
                {"head": partner},
            )

        def far_copy(b, c):
            span = spans[b][c]
            return remote(
                far_send.at[b, :, span],
                far_recv.at[b, :, span],
                far_send_sem,
                far_recv_sem.at[bases[b] + c],
                {"head": far},
            )

        def done_copy(b, c):
            span = spans[b][c]
            return remote(
                done_send.at[b, :, span],
                done_recv.at[s, :, span],
                done_send_sem,
                done_recv_sem.at[s],
                {"section": b},
            )

        def whole(ref, send_sem, recv_sem):
            return remote(ref, ref, send_sem, recv_sem, {"head": partner})


        def wait_kv_sent():
            for i, source in enumerate((k_v, v_v)):
                remote(
                    source, source, kv_send_sem.at[i], kv_recv_sem.at[0], {"section": s + 1}
                ).wait_send()

        def send_own(step, j):
            if s == 0 and not started:
                wait_kv_sent()
                pl.semaphore_signal(
                    cleared, inc=1, device_id={"head": partner}, device_id_type=MESH
                )
                pl.semaphore_wait(cleared, 1)
            started.append(parts_of(s))
            attn_copy(0, s, j, s + step).start()

        def relay(b, j):
            attn_copy(1, b, j, s).wait_recv()
            if b in onward:
                passed.append(parts_of(b))
                attn_copy(1, b, j, onward[b]).start()

        def multiply(b, j):
            left = jnp.concatenate(
                [
                    attn[b, pl.ds(pl.multiple_of(starts[j] + side * own_rows, own_rows), own_rows)]
                    for side in (1 - core, core)
                ],
                axis=0,
            )
            for c, span in enumerate(spans[b]):
                product = jnp.dot(left, w_t[:, span], preferred_element_type=jnp.float32)
                pair_send[b, j, :, span] = product[:own_rows].astype(jnp.bfloat16)
                mine[b, j, :, span] = product[own_rows:]
                pair_copy(b, j, c).start()

        def add_pair(b, c):
            span = spans[b][c]
            pair_copy(b, 0, c).wait_recv()
            far_send[b, :, span] = (
                mine[b, 0, :, span] + wide_of(pair_recv[b, 0, :, span])
            ).astype(jnp.bfloat16)
            far_copy(b, c).start()

        def add_far(b, c):
            span = spans[b][c]
            if b not in paired:
                paired.append(b)
                whole(
                    pair_send.at[b, 1], pair_send_sem, pair_recv_sem.at[bases[-1] + len(spans[-1]) + b]
                ).wait_recv()
            far_copy(b, c).wait_recv()
            value = (
                mine[b, 1, :, span]
                + wide_of(pair_recv[b, 1, :, span])
                + wide_of(far_recv[b, :, span])
            ).astype(jnp.bfloat16)
            if b == s:
                done_recv[s, :, span] = value
            else:
                done_send[b, :, span] = value
                done_copy(b, c).start()

        def gather(b, c):
            if b != s:
                whole(done_recv.at[b], done_send_sem, done_recv_sem.at[b]).wait_recv()
            value = wide_of(done_recv[b])
            squares.append(jnp.sum(value * value, axis=-1, keepdims=True))
            columns = slice(b * width, (b + 1) * width)
            scaled[:, columns] = value * gain_w[:, columns]

        actions = {
            "S": send_own,
            "R": relay,
            "M": multiply,
            "P": add_pair,
            "F": add_far,
            "N": gather,
        }
        for step in ORDERS[n][s]:
            kind, b, j = step[0], int(step[1:-1]), int(step[-1])
            actions[kind](b, j)
        scale = lax.rsqrt(sum(squares) / (n * width) + norm_eps)
        out_ref[...] = (wide_of(res_v[...]) + scaled[...] * scale).astype(out_ref.dtype)

        if s != 0 and s + 1 < n:
            wait_kv_sent()
        for slot, sent in enumerate((started, passed)):
            if sent:
                half = attn.at[0 : round(sum(1 / parts for parts in sent))]
                whole(half, attn_send_sem.at[slot], attn_recv_sem.at[0]).wait_send()
        whole(pair_send, pair_send_sem, pair_recv_sem.at[0]).wait_send()
        whole(far_send, far_send_sem, far_recv_sem.at[0]).wait_send()
        whole(done_send.at[: n - 1], done_send_sem, done_recv_sem.at[s]).wait_send()

    for s in range(n):

        @pl.when(me == s)
        def _(s=s):
            run(s)


def fused_local(
    n, heads, queries, token_key_rows, token_value_rows, residual, prefix, out_weight, post_gain
):
    rows = queries.shape[0]
    own_rows = rows // heads
    width = out_weight.shape[1]
    key_heads = token_key_rows.shape[1] // HEAD_SIZE
    low = jnp.bfloat16
    stays = pl.BlockSpec(memory_space=pltpu.HBM)
    vector = pl.BlockSpec(memory_space=pltpu.VMEM)
    dma = pltpu.SemaphoreType.DMA
    weights = out_weight.T
    part = (n, own_rows, width)
    pieces = max(sum(pieces_of(s, b, n) for b in range(n)) for s in range(n))
    return pl.pallas_call(
        functools.partial(fused_kernel, n, heads),
        out_shape=pltpu.VMEM(residual.shape, low),
        in_specs=[stays] * 7,
        out_specs=vector,
        scratch_shapes=[
            pltpu.SMEM(prefix.shape, jnp.int32),
            pltpu.VMEM(queries.shape, low),
            pltpu.VMEM(token_key_rows.shape, low),
            pltpu.VMEM(token_value_rows.shape, low),
            pltpu.VMEM(token_key_rows.shape, low),
            pltpu.VMEM(token_value_rows.shape, low),
            pltpu.VMEM(weights.shape, low),
            pltpu.VMEM(out_weight.shape, low),
            pltpu.VMEM(residual.shape, low),
            pltpu.VMEM(post_gain.shape, jnp.float32),
            pltpu.VMEM((own_rows,) + post_gain.shape, jnp.float32),
            pltpu.VMEM((n, rows, queries.shape[1]), low),
            pltpu.VMEM((n, 2, own_rows, width), low),
            pltpu.VMEM((n, 2, own_rows, width), low),
            pltpu.VMEM((n, 2, own_rows, width), jnp.float32),
            pltpu.VMEM(part, low),
            pltpu.VMEM(part, low),
            pltpu.VMEM(part, low),
            pltpu.VMEM(part, low),
            pltpu.VMEM(residual.shape, jnp.float32),
            dma((7,)),
            dma((2,)),
            dma((key_heads,)),
            dma((2,)),
            dma((2 * n + 4,)),
            dma,
            dma((pieces + n,)),
            dma,
            dma((pieces,)),
            dma,
            dma((n,)),
            pltpu.SemaphoreType.REGULAR,
        ],
        compiler_params=pltpu.CompilerParams(
            collective_id=0, has_side_effects=True, vmem_limit_bytes=VMEM_LIMIT
        ),
    )(prefix, queries, token_key_rows, token_value_rows, weights, residual, post_gain)


def shifted(value, axis, steps):
    count = lax.axis_size(axis)
    leading, last = (max(0, -steps), min(count, count - steps))
    return lax.ppermute(value, axis, [(source, source + steps) for source in range(leading, last)])


def empty_state(row_count, key_heads, group_width):
    running_max = jnp.full((key_heads, group_width, row_count), floor_value, jnp.float32)
    running_sum = jnp.zeros((key_heads, group_width, row_count), jnp.float32)
    weighted = jnp.zeros((row_count, key_heads, group_width, HEAD_SIZE), jnp.float32)
    return (running_max, running_sum, weighted)


def attend(
    status, query_tile_block, query_pos, lower_pos, key_tile_block, value_tile_block, key_pos
):
    running_max, running_sum, weighted = status
    row_count = query_tile_block.shape[0]
    key_heads = key_tile_block.shape[1] // HEAD_SIZE
    group_width = query_tile_block.shape[1] // (key_heads * HEAD_SIZE)
    query_four = query_tile_block.reshape(row_count, key_heads, group_width, HEAD_SIZE)
    key_three = key_tile_block.reshape(key_tile_block.shape[0], key_heads, HEAD_SIZE)
    value_three = value_tile_block.reshape(value_tile_block.shape[0], key_heads, HEAD_SIZE)
    scores = (
        jnp.einsum("qkgd,pkd->kgqp", query_four, key_three, preferred_element_type=jnp.float32)
        * score_scale
    )
    visible = (key_pos[None, :] <= query_pos[:, None]) & (key_pos[None, :] >= lower_pos)
    masked = jnp.where(visible, scores, floor_value)
    new_max = jnp.maximum(running_max, jnp.max(masked, axis=-1))
    carry_scale = jnp.exp(running_max - new_max)
    weights = jnp.where(visible, jnp.exp(masked - new_max[..., None]), 0.0)
    running_sum = carry_scale * running_sum + jnp.sum(weights, axis=-1)
    product = jnp.einsum(
        "kgqp,pkd->qkgd",
        weights.astype(jnp.bfloat16),
        value_three,
        preferred_element_type=jnp.float32,
    )
    weighted = jnp.transpose(carry_scale, (2, 0, 1))[..., None] * weighted + product
    return (new_max, running_sum, weighted)


def local(queries, token_key_rows, token_value_rows, residual, prefix, out_weight, post_gain):
    row_count = queries.shape[0]
    key_heads = token_key_rows.shape[1] // HEAD_SIZE
    group_width = queries.shape[1] // (key_heads * HEAD_SIZE)
    section_total = lax.axis_size("section")
    section_index = lax.axis_index("section")
    reachable_blocks = 3 * section_total // 8
    base_rows = jnp.arange(row_count, dtype=jnp.int32)
    own_pos = section_index * row_count + base_rows
    seen_tokens = jnp.minimum(section_index * row_count, prefix[section_index])
    lower_pos = section_index * row_count - seen_tokens
    block_count = (seen_tokens + row_count - 1) // row_count
    blank = empty_state(row_count, key_heads, group_width)
    states = attend(blank, queries, own_pos, lower_pos, token_key_rows, token_value_rows, own_pos)

    def process(distance, key_tile_block, value_tile_block, mine):
        key_pos = (section_index - distance) * row_count + base_rows
        use_mine = distance <= block_count
        return lax.cond(
            use_mine,
            lambda current: attend(
                current, queries, own_pos, lower_pos, key_tile_block, value_tile_block, key_pos
            ),
            lambda current: current,
            mine,
        )

    held_keys = token_key_rows[None]
    held_values = token_value_rows[None]
    stride = 1
    while stride <= reachable_blocks:
        amount_moved = min(stride, reachable_blocks + 1 - stride)
        moved_keys, moved_values = shifted(
            (held_keys[:amount_moved], held_values[:amount_moved]), "section", stride
        )
        held_keys = jnp.concatenate([held_keys, moved_keys], axis=0)
        held_values = jnp.concatenate([held_values, moved_values], axis=0)
        stride = stride * 2

    def visit_block(distance, inner):
        key_tile_block = lax.dynamic_index_in_dim(held_keys, distance, 0, keepdims=False)
        value_tile_block = lax.dynamic_index_in_dim(held_values, distance, 0, keepdims=False)
        return process(distance, key_tile_block, value_tile_block, inner)

    states = lax.fori_loop(1, reachable_blocks + 1, visit_block, states)
    attention = states[2] / jnp.transpose(states[1], (2, 0, 1))[..., None]
    attention = attention.reshape(row_count, key_heads * group_width * HEAD_SIZE).astype(
        jnp.bfloat16
    )
    partial_out = jnp.dot(
        attention,
        lax.all_gather(out_weight, "section", axis=1, tiled=True),
        preferred_element_type=jnp.float32,
    )
    summed = lax.psum_scatter(
        partial_out.astype(jnp.bfloat16), "head", scatter_dimension=0, tiled=True
    ).astype(jnp.float32)
    mean_square = jnp.mean(summed * summed, axis=-1, keepdims=True)
    normed = summed * lax.rsqrt(mean_square + norm_eps) * post_gain[None, :]
    return (residual.astype(jnp.float32) + normed).astype(jnp.bfloat16)


def solution(mesh):
    placed = (
        P(("groups", "section"), "head"),
        P(("groups", "section"), "head"),
        P(("groups", "section"), "head"),
        P(("groups", "section", "head"), None),
        P("groups"),
        P("head", "section"),
        P(),
    )
    n, heads = mesh.shape["section"], mesh.shape["head"]
    body = local
    if n in ORDERS and 3 * n // 8 == 1 and heads == 4:
        body = functools.partial(fused_local, n, heads)
    return jax.shard_map(
        body,
        mesh=mesh,
        in_specs=placed,
        out_specs=P(("groups", "section", "head"), None),
        check_vma=False,
    )
```

```python
import functools

import jax
import jax.numpy as jnp
from jax import lax
from jax.experimental import pallas as pl
from jax.experimental.pallas import tpu as pltpu
from jax.sharding import PartitionSpec as P

HEAD_SIZE = 128


score_scale = 168.0 ** (-0.5)
floor_value = -1e30
norm_eps = 1e-06
LANES = 128
FARTHER = 1
VMEM_LIMIT = (60 * 1024 - 720) * 1024
MESH = pl.DeviceIdType.MESH


ORDERS = {
    4: (
        (
            "M00", "M01", "S10", "S11", "S12", "S13", "P00", "R10", "M10", "R11", "P10", "P11",
            "M11", "R20", "M20", "R21", "P20", "P21", "M21", "F10", "F11", "R30", "R31", "M30",
            "P30", "P31", "F20", "R32", "F21", "R33", "M31", "F30", "F31", "F00", "N00", "N10",
            "N20", "N30",
        ),
        (
            "S-10", "S10", "S-11", "S11", "M10", "M11", "P10", "R00", "R01", "M00", "R02", "R03",
            "P00", "P01", "R20", "M20", "R21", "P20", "P21", "M01", "M21", "R30", "R31", "M30",
            "R32", "P30", "P31", "R33", "M31", "F00", "F01", "F20", "F21", "F30", "F31", "F10",
            "N10", "N00", "N20", "N30",
        ),
        (
            "S-10", "S10", "S-11", "S11", "M20", "M21", "P20", "R10", "M10", "R30", "R31", "P10",
            "P11", "R00", "R32", "R01", "M00", "R33", "P00", "P01", "R02", "R03", "R11", "M11",
            "M01", "F10", "F11", "M30", "P30", "P31", "M31", "F00", "F01", "F30", "F31", "F20",
            "N20", "N30", "N10", "N00",
        ),
        (
            "S-10", "S-11", "S-12", "S-13", "M30", "M31", "P30", "R20", "M20", "P20", "P21",
            "R21", "M21", "R00", "R01", "M00", "P00", "P01", "R10", "M10", "R02", "R03", "M01",
            "P10", "P11", "F20", "F21", "F00", "F01", "R11", "M11", "F10", "F11", "F30", "N30",
            "N20", "N10", "N00",
        ),
    ),
}


def pieces_of(s, b, n):
    return 1 if abs(b - s) < FARTHER else 2


def fused_kernel(
    n,
    heads,
    prefix_hbm,
    q_hbm,
    k_hbm,
    v_hbm,
    w_hbm,
    res_hbm,
    gain_hbm,
    out_ref,
    prefix_ref,
    q_v,
    k_v,
    v_v,
    k_prev,
    v_prev,
    w_v,
    w_t,
    res_v,
    gain_v,
    gain_w,
    attn,
    pair_send,
    pair_recv,
    mine,
    far_send,
    far_recv,
    done_send,
    done_recv,
    scaled,
    load_sem,
    kv_send_sem,
    kv_recv_sem,
    send_sem,
    attn_recv_sem,
    pair_recv_sem,
    far_recv_sem,
    done_recv_sem,
    cleared,
):
    me = lax.axis_index("section")
    h = lax.axis_index("head")
    rows = q_hbm.shape[0]
    own_rows = rows // heads
    core = lax.rem(h, 2)
    partner = h + 1 - 2 * core
    far = lax.rem(h + 2, heads)
    group_rows = 2 * own_rows
    starts = [
        pl.multiple_of(lax.rem(h // 2 + 1 + j, 2) * group_rows, group_rows) for j in range(2)
    ]
    key_heads = k_hbm.shape[1] // HEAD_SIZE
    group_width = q_hbm.shape[1] // k_hbm.shape[1]
    width = w_hbm.shape[0]

    def cut(count):
        edges = [LANES * round(width * c / (count * LANES)) for c in range(count)] + [width]
        return [slice(a, b) for a, b in zip(edges, edges[1:])]

    def remote(source, target, send_sem, recv_sem, where):
        return pltpu.make_async_remote_copy(
            src_ref=source,
            dst_ref=target,
            send_sem=send_sem,
            recv_sem=recv_sem,
            device_id=where,
            device_id_type=MESH,
        )

    loads = [
        pltpu.make_async_copy(source, target, load_sem.at[(i + 2) // 3])
        for i, (source, target) in enumerate(
            (
                (prefix_hbm, prefix_ref),
                (q_hbm, q_v),
                (k_hbm, k_v),
                (v_hbm, v_v),
                (w_hbm, w_v),
                (res_hbm, res_v),
                (gain_hbm, gain_v),
            )
        )
    ]
    has_below, has_above = me > 0, me + 1 < n
    barrier = pltpu.get_barrier_semaphore()
    for there, step in ((has_below, -1), (has_above, 1)):

        @pl.when(there)
        def _(step=step):
            pl.semaphore_signal(
                barrier, inc=1, device_id={"section": me + step}, device_id_type=MESH
            )

    for other in (partner, far):
        pl.semaphore_signal(barrier, inc=1, device_id={"head": other}, device_id_type=MESH)
    for load in loads:
        load.start()
    for load in loads[:4]:
        load.wait()
    pl.semaphore_wait(
        barrier, 2 + jnp.where(has_below, 1, 0) + jnp.where(has_above, 1, 0)
    )

    def head_span(at):
        return slice(at * HEAD_SIZE, (at + 1) * HEAD_SIZE)

    def kv_copies():
        return [
            remote(
                source,
                target,
                kv_send_sem,
                kv_recv_sem.at[i],
                {"section": lax.rem(me + 1, n)},
            )
            for i, (source, target) in enumerate(((k_v, k_prev), (v_v, v_prev)))
        ]

    @pl.when(has_above)
    def _():
        for copy in kv_copies():
            copy.start()

    @pl.when(me == 0)
    def _():
        k_prev[...] = jnp.zeros_like(k_prev)
        v_prev[...] = jnp.zeros_like(v_prev)

    seen = jnp.minimum(me * rows, prefix_ref[me])
    wide = group_width * rows
    q_row = lax.rem(lax.broadcasted_iota(jnp.int32, (wide, rows), 0), rows)
    k_col = lax.broadcasted_iota(jnp.int32, (wide, rows), 1)
    own_seen = k_col <= q_row
    prev_seen = k_col >= rows - seen

    def head_columns(ref, at):
        return ref[:, head_span(at)]

    def scores_of(query, key):
        return (
            lax.dot_general(
                query, key, (((1,), (1,)), ((), ())), preferred_element_type=jnp.float32
            )
            * score_scale
        )

    queries = [
        jnp.concatenate(
            [head_columns(q_v, kh * group_width + g) for g in range(group_width)], axis=0
        )
        for kh in range(key_heads)
    ]
    own_parts = []
    for kh in range(key_heads):
        own = jnp.where(own_seen, scores_of(queries[kh], head_columns(k_v, kh)), floor_value)
        own_top = jnp.max(own, axis=-1, keepdims=True)
        own_probs = jnp.where(own_seen, jnp.exp(own - own_top), 0.0)
        own_total = jnp.sum(own_probs, axis=-1, keepdims=True)
        own_combined = jnp.dot(
            own_probs.astype(jnp.bfloat16),
            head_columns(v_v, kh),
            preferred_element_type=jnp.float32,
        )
        own_parts.append((own_top, own_total, own_combined))

    for load in loads[4:]:
        load.wait()
    w_t[...] = w_v[...].T
    gain_w[...] = jnp.broadcast_to(gain_v[...][None, :], gain_w.shape)

    @pl.when(has_below)
    def _():
        kv_copies()[0].wait_recv()

    joined = []
    for kh in range(key_heads):
        own_top, own_total, own_combined = own_parts[kh]
        prev = jnp.where(
            prev_seen, scores_of(queries[kh], head_columns(k_prev, kh)), floor_value
        )
        top = jnp.maximum(own_top, jnp.max(prev, axis=-1, keepdims=True))
        prev_probs = jnp.where(prev_seen, jnp.exp(prev - top), 0.0)
        carry = jnp.exp(own_top - top)
        inverse = 1.0 / (carry * own_total + jnp.sum(prev_probs, axis=-1, keepdims=True))
        joined.append((prev_probs.astype(jnp.bfloat16), carry * own_combined, inverse))

    @pl.when(has_below)
    def _():
        kv_copies()[1].wait_recv()

    for kh in range(key_heads):
        prev_probs, own_combined, inverse = joined[kh]
        combined = own_combined + jnp.dot(
            prev_probs, head_columns(v_prev, kh), preferred_element_type=jnp.float32
        )
        result = (combined * inverse).astype(jnp.bfloat16)
        for g in range(group_width):
            attn[me, :, head_span(kh * group_width + g)] = result[g * rows : (g + 1) * rows]

    def parts_of(block):
        return 4 if block in (0, n - 1) else 2

    def attn_copy(slot, block, j, target):
        count = 2 * group_rows // parts_of(block)
        half, at = divmod(j * count, group_rows)
        here = attn.at[block, pl.ds(pl.multiple_of(starts[half] + at, count), count)]
        return remote(
            here,
            here,
            send_sem,
            attn_recv_sem.at[sum(parts_of(b) for b in range(block)) + j],
            {"section": target},
        )

    def wide_of(block):
        return block.astype(jnp.float32)

    def run(s):
        onward = {b: (s + 1 if b < s else s - 1) for b in range(n) if b != s}
        onward = {b: t for b, t in onward.items() if 0 <= t < n}
        squares = []
        started, passed, paired = [], [], []

        spans = [cut(pieces_of(s, b, n)) for b in range(n)]
        bases = [sum(map(len, spans[:b])) for b in range(n)]

        def pair_copy(b, j, c):
            span = spans[b][c]
            at = bases[b] + c if j == 0 else bases[-1] + len(spans[-1]) + b
            return remote(
                pair_send.at[b, j, :, span],
                pair_recv.at[b, j, :, span],
                send_sem,
                pair_recv_sem.at[at],
                {"head": partner},
            )

        def far_copy(b, c):
            span = spans[b][c]
            return remote(
                far_send.at[b, :, span],
                far_recv.at[b, :, span],
                send_sem,
                far_recv_sem.at[bases[b] + c],
                {"head": far},
            )

        def done_copy(b, c):
            span = spans[b][c]
            return remote(
                done_send.at[b, :, span],
                done_recv.at[s, :, span],
                send_sem,
                done_recv_sem.at[s],
                {"section": b},
            )

        def whole(ref, send_sem, recv_sem):
            return remote(ref, ref, send_sem, recv_sem, {"head": partner})


        def wait_kv_sent():
            for i, source in enumerate((k_v, v_v)):
                remote(
                    source, source, kv_send_sem, kv_recv_sem.at[0], {"section": s + 1}
                ).wait_send()

        def send_own(step, j):
            if s == 0 and not started:
                wait_kv_sent()
                pl.semaphore_signal(
                    cleared, inc=1, device_id={"head": partner}, device_id_type=MESH
                )
                pl.semaphore_wait(cleared, 1)
            started.append(parts_of(s))
            attn_copy(0, s, j, s + step).start()

        def relay(b, j):
            attn_copy(1, b, j, s).wait_recv()
            if b in onward:
                passed.append(parts_of(b))
                attn_copy(1, b, j, onward[b]).start()

        def multiply(b, j):
            left = jnp.concatenate(
                [
                    attn[b, pl.ds(pl.multiple_of(starts[j] + side * own_rows, own_rows), own_rows)]
                    for side in (1 - core, core)
                ],
                axis=0,
            )
            for c, span in enumerate(spans[b]):
                product = jnp.dot(left, w_t[:, span], preferred_element_type=jnp.float32)
                pair_send[b, j, :, span] = product[:own_rows].astype(jnp.bfloat16)
                mine[b, j, :, span] = product[own_rows:]
                pair_copy(b, j, c).start()

        def add_pair(b, c):
            span = spans[b][c]
            pair_copy(b, 0, c).wait_recv()
            far_send[b, :, span] = (
                mine[b, 0, :, span] + wide_of(pair_recv[b, 0, :, span])
            ).astype(jnp.bfloat16)
            far_copy(b, c).start()

        def add_far(b, c):
            span = spans[b][c]
            if b not in paired:
                paired.append(b)
                whole(
                    pair_send.at[b, 1], send_sem, pair_recv_sem.at[bases[-1] + len(spans[-1]) + b]
                ).wait_recv()
            far_copy(b, c).wait_recv()
            value = (
                mine[b, 1, :, span]
                + wide_of(pair_recv[b, 1, :, span])
                + wide_of(far_recv[b, :, span])
            ).astype(jnp.bfloat16)
            if b == s:
                done_recv[s, :, span] = value
            else:
                done_send[b, :, span] = value
                done_copy(b, c).start()

        def gather(b, c):
            if b != s:
                whole(done_recv.at[b], send_sem, done_recv_sem.at[b]).wait_recv()
            value = wide_of(done_recv[b])
            squares.append(jnp.sum(value * value, axis=-1, keepdims=True))
            columns = slice(b * width, (b + 1) * width)
            scaled[:, columns] = value * gain_w[:, columns]

        actions = {
            "S": send_own,
            "R": relay,
            "M": multiply,
            "P": add_pair,
            "F": add_far,
            "N": gather,
        }
        for step in ORDERS[n][s]:
            kind, b, j = step[0], int(step[1:-1]), int(step[-1])
            actions[kind](b, j)
        scale = lax.rsqrt(sum(squares) / (n * width) + norm_eps)
        out_ref[...] = (wide_of(res_v[...]) + scaled[...] * scale).astype(out_ref.dtype)

        if s != 0 and s + 1 < n:
            wait_kv_sent()
        for slot, sent in enumerate((started, passed)):
            if sent:
                half = attn.at[0 : round(sum(1 / parts for parts in sent))]
                whole(half, send_sem, attn_recv_sem.at[0]).wait_send()
        whole(pair_send, send_sem, pair_recv_sem.at[0]).wait_send()
        whole(far_send, send_sem, far_recv_sem.at[0]).wait_send()
        whole(done_send.at[: n - 1], send_sem, done_recv_sem.at[s]).wait_send()

    for s in range(n):

        @pl.when(me == s)
        def _(s=s):
            run(s)


def fused_local(
    n, heads, queries, token_key_rows, token_value_rows, residual, prefix, out_weight, post_gain
):
    rows = queries.shape[0]
    own_rows = rows // heads
    width = out_weight.shape[1]
    key_heads = token_key_rows.shape[1] // HEAD_SIZE
    low = jnp.bfloat16
    stays = pl.BlockSpec(memory_space=pltpu.HBM)
    vector = pl.BlockSpec(memory_space=pltpu.VMEM)
    dma = pltpu.SemaphoreType.DMA
    weights = out_weight.T
    part = (n, own_rows, width)
    pieces = max(sum(pieces_of(s, b, n) for b in range(n)) for s in range(n))
    return pl.pallas_call(
        functools.partial(fused_kernel, n, heads),
        out_shape=pltpu.VMEM(residual.shape, low),
        in_specs=[stays] * 7,
        out_specs=vector,
        scratch_shapes=[
            pltpu.SMEM(prefix.shape, jnp.int32),
            pltpu.VMEM(queries.shape, low),
            pltpu.VMEM(token_key_rows.shape, low),
            pltpu.VMEM(token_value_rows.shape, low),
            pltpu.VMEM(token_key_rows.shape, low),
            pltpu.VMEM(token_value_rows.shape, low),
            pltpu.VMEM(weights.shape, low),
            pltpu.VMEM(out_weight.shape, low),
            pltpu.VMEM(residual.shape, low),
            pltpu.VMEM(post_gain.shape, jnp.float32),
            pltpu.VMEM((own_rows,) + post_gain.shape, jnp.float32),
            pltpu.VMEM((n, rows, queries.shape[1]), low),
            pltpu.VMEM((n, 2, own_rows, width), low),
            pltpu.VMEM((n, 2, own_rows, width), low),
            pltpu.VMEM((n, 2, own_rows, width), jnp.float32),
            pltpu.VMEM(part, low),
            pltpu.VMEM(part, low),
            pltpu.VMEM(part, low),
            pltpu.VMEM(part, low),
            pltpu.VMEM(residual.shape, jnp.float32),
            dma((3,)),
            dma,
            dma((2,)),
            dma,
            dma((2 * n + 4,)),
            dma((pieces + n,)),
            dma((pieces,)),
            dma((n,)),
            pltpu.SemaphoreType.REGULAR,
        ],
        compiler_params=pltpu.CompilerParams(
            collective_id=0, has_side_effects=True, vmem_limit_bytes=VMEM_LIMIT
        ),
    )(prefix, queries, token_key_rows, token_value_rows, weights, residual, post_gain)


def shifted(value, axis, steps):
    count = lax.axis_size(axis)
    leading, last = (max(0, -steps), min(count, count - steps))
    return lax.ppermute(value, axis, [(source, source + steps) for source in range(leading, last)])


def empty_state(row_count, key_heads, group_width):
    running_max = jnp.full((key_heads, group_width, row_count), floor_value, jnp.float32)
    running_sum = jnp.zeros((key_heads, group_width, row_count), jnp.float32)
    weighted = jnp.zeros((row_count, key_heads, group_width, HEAD_SIZE), jnp.float32)
    return (running_max, running_sum, weighted)


def attend(
    status, query_tile_block, query_pos, lower_pos, key_tile_block, value_tile_block, key_pos
):
    running_max, running_sum, weighted = status
    row_count = query_tile_block.shape[0]
    key_heads = key_tile_block.shape[1] // HEAD_SIZE
    group_width = query_tile_block.shape[1] // (key_heads * HEAD_SIZE)
    query_four = query_tile_block.reshape(row_count, key_heads, group_width, HEAD_SIZE)
    key_three = key_tile_block.reshape(key_tile_block.shape[0], key_heads, HEAD_SIZE)
    value_three = value_tile_block.reshape(value_tile_block.shape[0], key_heads, HEAD_SIZE)
    scores = (
        jnp.einsum("qkgd,pkd->kgqp", query_four, key_three, preferred_element_type=jnp.float32)
        * score_scale
    )
    visible = (key_pos[None, :] <= query_pos[:, None]) & (key_pos[None, :] >= lower_pos)
    masked = jnp.where(visible, scores, floor_value)
    new_max = jnp.maximum(running_max, jnp.max(masked, axis=-1))
    carry_scale = jnp.exp(running_max - new_max)
    weights = jnp.where(visible, jnp.exp(masked - new_max[..., None]), 0.0)
    running_sum = carry_scale * running_sum + jnp.sum(weights, axis=-1)
    product = jnp.einsum(
        "kgqp,pkd->qkgd",
        weights.astype(jnp.bfloat16),
        value_three,
        preferred_element_type=jnp.float32,
    )
    weighted = jnp.transpose(carry_scale, (2, 0, 1))[..., None] * weighted + product
    return (new_max, running_sum, weighted)


def local(queries, token_key_rows, token_value_rows, residual, prefix, out_weight, post_gain):
    row_count = queries.shape[0]
    key_heads = token_key_rows.shape[1] // HEAD_SIZE
    group_width = queries.shape[1] // (key_heads * HEAD_SIZE)
    section_total = lax.axis_size("section")
    section_index = lax.axis_index("section")
    reachable_blocks = 3 * section_total // 8
    base_rows = jnp.arange(row_count, dtype=jnp.int32)
    own_pos = section_index * row_count + base_rows
    seen_tokens = jnp.minimum(section_index * row_count, prefix[section_index])
    lower_pos = section_index * row_count - seen_tokens
    block_count = (seen_tokens + row_count - 1) // row_count
    blank = empty_state(row_count, key_heads, group_width)
    states = attend(blank, queries, own_pos, lower_pos, token_key_rows, token_value_rows, own_pos)

    def process(distance, key_tile_block, value_tile_block, mine):
        key_pos = (section_index - distance) * row_count + base_rows
        use_mine = distance <= block_count
        return lax.cond(
            use_mine,
            lambda current: attend(
                current, queries, own_pos, lower_pos, key_tile_block, value_tile_block, key_pos
            ),
            lambda current: current,
            mine,
        )

    held_keys = token_key_rows[None]
    held_values = token_value_rows[None]
    stride = 1
    while stride <= reachable_blocks:
        amount_moved = min(stride, reachable_blocks + 1 - stride)
        moved_keys, moved_values = shifted(
            (held_keys[:amount_moved], held_values[:amount_moved]), "section", stride
        )
        held_keys = jnp.concatenate([held_keys, moved_keys], axis=0)
        held_values = jnp.concatenate([held_values, moved_values], axis=0)
        stride = stride * 2

    def visit_block(distance, inner):
        key_tile_block = lax.dynamic_index_in_dim(held_keys, distance, 0, keepdims=False)
        value_tile_block = lax.dynamic_index_in_dim(held_values, distance, 0, keepdims=False)
        return process(distance, key_tile_block, value_tile_block, inner)

    states = lax.fori_loop(1, reachable_blocks + 1, visit_block, states)
    attention = states[2] / jnp.transpose(states[1], (2, 0, 1))[..., None]
    attention = attention.reshape(row_count, key_heads * group_width * HEAD_SIZE).astype(
        jnp.bfloat16
    )
    partial_out = jnp.dot(
        attention,
        lax.all_gather(out_weight, "section", axis=1, tiled=True),
        preferred_element_type=jnp.float32,
    )
    summed = lax.psum_scatter(
        partial_out.astype(jnp.bfloat16), "head", scatter_dimension=0, tiled=True
    ).astype(jnp.float32)
    mean_square = jnp.mean(summed * summed, axis=-1, keepdims=True)
    normed = summed * lax.rsqrt(mean_square + norm_eps) * post_gain[None, :]
    return (residual.astype(jnp.float32) + normed).astype(jnp.bfloat16)


def solution(mesh):
    placed = (
        P(("groups", "section"), "head"),
        P(("groups", "section"), "head"),
        P(("groups", "section"), "head"),
        P(("groups", "section", "head"), None),
        P("groups"),
        P("head", "section"),
        P(),
    )
    n, heads = mesh.shape["section"], mesh.shape["head"]
    body = local
    if n in ORDERS and 3 * n // 8 == 1 and heads == 4:
        body = functools.partial(fused_local, n, heads)
    return jax.shard_map(
        body,
        mesh=mesh,
        in_specs=placed,
        out_specs=P(("groups", "section", "head"), None),
        check_vma=False,
    )
```

```python
import functools

import jax
import jax.numpy as jnp
from jax import lax
from jax.experimental import pallas as pl
from jax.experimental.pallas import tpu as pltpu
from jax.sharding import PartitionSpec as P

HEAD_SIZE = 128


score_scale = 168.0 ** (-0.5)
floor_value = -1e30
norm_eps = 1e-06
LANES = 128
FARTHER = 1
VMEM_LIMIT = (60 * 1024 - 720) * 1024
MESH = pl.DeviceIdType.MESH


ORDERS = {
    4: (
        (
            "M00", "M01", "S10", "S11", "S12", "S13", "P00", "R10", "M10", "R11", "P10", "P11",
            "M11", "R20", "M20", "R21", "P20", "P21", "M21", "F10", "F11", "R30", "R31", "M30",
            "P30", "P31", "F20", "R32", "F21", "R33", "M31", "F30", "F31", "F00", "N00", "N10",
            "N20", "N30",
        ),
        (
            "S-10", "S10", "S-11", "S11", "M10", "M11", "P10", "R00", "R01", "M00", "R02", "R03",
            "P00", "P01", "R20", "M20", "R21", "P20", "P21", "M01", "M21", "R30", "R31", "M30",
            "R32", "P30", "P31", "R33", "M31", "F00", "F01", "F20", "F21", "F30", "F31", "F10",
            "N10", "N00", "N20", "N30",
        ),
        (
            "S-10", "S10", "S-11", "S11", "M20", "M21", "P20", "R10", "M10", "R30", "R31", "P10",
            "P11", "R00", "R32", "R01", "M00", "R33", "P00", "P01", "R02", "R03", "R11", "M11",
            "M01", "F10", "F11", "M30", "P30", "P31", "M31", "F00", "F01", "F30", "F31", "F20",
            "N20", "N30", "N10", "N00",
        ),
        (
            "S-10", "S-11", "S-12", "S-13", "M30", "M31", "P30", "R20", "M20", "P20", "P21",
            "R21", "M21", "R00", "R01", "M00", "P00", "P01", "R10", "M10", "F20", "F21", "R02",
            "R03", "M01", "P10", "P11", "F00", "F01", "R11", "M11", "F10", "F11", "F30", "N30",
            "N20", "N10", "N00",
        ),
    ),
}


def pieces_of(s, b, n):
    return 1 if abs(b - s) < FARTHER else 2


def fused_kernel(
    n,
    heads,
    prefix_hbm,
    q_hbm,
    k_hbm,
    v_hbm,
    w_hbm,
    res_hbm,
    gain_hbm,
    out_ref,
    prefix_ref,
    q_v,
    k_v,
    v_v,
    k_prev,
    v_prev,
    w_v,
    w_t,
    res_v,
    gain_v,
    gain_w,
    attn,
    pair_send,
    pair_recv,
    mine,
    far_send,
    far_recv,
    done_send,
    done_recv,
    scaled,
    load_sem,
    kv_send_sem,
    kv_recv_sem,
    send_sem,
    attn_recv_sem,
    pair_recv_sem,
    far_recv_sem,
    done_recv_sem,
    cleared,
):
    me = lax.axis_index("section")
    h = lax.axis_index("head")
    rows = q_hbm.shape[0]
    own_rows = rows // heads
    core = lax.rem(h, 2)
    partner = h + 1 - 2 * core
    far = lax.rem(h + 2, heads)
    group_rows = 2 * own_rows
    starts = [
        pl.multiple_of(lax.rem(h // 2 + 1 + j, 2) * group_rows, group_rows) for j in range(2)
    ]
    key_heads = k_hbm.shape[1] // HEAD_SIZE
    group_width = q_hbm.shape[1] // k_hbm.shape[1]
    width = w_hbm.shape[0]

    def cut(count):
        edges = [LANES * round(width * c / (count * LANES)) for c in range(count)] + [width]
        return [slice(a, b) for a, b in zip(edges, edges[1:])]

    def remote(source, target, send_sem, recv_sem, where):
        return pltpu.make_async_remote_copy(
            src_ref=source,
            dst_ref=target,
            send_sem=send_sem,
            recv_sem=recv_sem,
            device_id=where,
            device_id_type=MESH,
        )

    loads = [
        pltpu.make_async_copy(source, target, load_sem.at[(i + 2) // 3])
        for i, (source, target) in enumerate(
            (
                (prefix_hbm, prefix_ref),
                (q_hbm, q_v),
                (k_hbm, k_v),
                (v_hbm, v_v),
                (w_hbm, w_v),
                (res_hbm, res_v),
                (gain_hbm, gain_v),
            )
        )
    ]
    has_below, has_above = me > 0, me + 1 < n
    barrier = pltpu.get_barrier_semaphore()
    for there, step in ((has_below, -1), (has_above, 1)):

        @pl.when(there)
        def _(step=step):
            pl.semaphore_signal(
                barrier, inc=1, device_id={"section": me + step}, device_id_type=MESH
            )

    for other in (partner, far):
        pl.semaphore_signal(barrier, inc=1, device_id={"head": other}, device_id_type=MESH)
    for load in loads:
        load.start()
    for load in loads[:4]:
        load.wait()
    pl.semaphore_wait(
        barrier, 2 + jnp.where(has_below, 1, 0) + jnp.where(has_above, 1, 0)
    )

    def head_span(at):
        return slice(at * HEAD_SIZE, (at + 1) * HEAD_SIZE)

    def kv_copy(i):
        source, target = ((k_v, k_prev), (v_v, v_prev))[i]
        above = {"section": lax.rem(me + 1, n)}
        return remote(source, target, kv_send_sem, kv_recv_sem.at[i], above)

    @pl.when(has_above)
    def _():
        for i in range(2):
            kv_copy(i).start()

    @pl.when(me == 0)
    def _():
        k_prev[...] = jnp.zeros_like(k_prev)
        v_prev[...] = jnp.zeros_like(v_prev)

    seen = jnp.minimum(me * rows, prefix_ref[me])
    wide = group_width * rows
    q_row = lax.rem(lax.broadcasted_iota(jnp.int32, (wide, rows), 0), rows)
    k_col = lax.broadcasted_iota(jnp.int32, (wide, rows), 1)
    own_seen = k_col <= q_row
    prev_seen = k_col >= rows - seen

    def head_columns(ref, at):
        return ref[:, head_span(at)]

    def scores_of(query, key):
        return (
            lax.dot_general(
                query, key, (((1,), (1,)), ((), ())), preferred_element_type=jnp.float32
            )
            * score_scale
        )

    queries = [
        jnp.concatenate(
            [head_columns(q_v, kh * group_width + g) for g in range(group_width)], axis=0
        )
        for kh in range(key_heads)
    ]
    own_parts = []
    for kh in range(key_heads):
        own = jnp.where(own_seen, scores_of(queries[kh], head_columns(k_v, kh)), floor_value)
        own_top = jnp.max(own, axis=-1, keepdims=True)
        own_probs = jnp.where(own_seen, jnp.exp(own - own_top), 0.0)
        own_total = jnp.sum(own_probs, axis=-1, keepdims=True)
        own_combined = jnp.dot(
            own_probs.astype(jnp.bfloat16),
            head_columns(v_v, kh),
            preferred_element_type=jnp.float32,
        )
        own_parts.append((own_top, own_total, own_combined))

    for load in loads[4:]:
        load.wait()
    w_t[...] = w_v[...].T
    gain_w[...] = jnp.broadcast_to(gain_v[...][None, :], gain_w.shape)

    @pl.when(has_below)
    def _():
        kv_copy(0).wait_recv()

    joined = []
    for kh in range(key_heads):
        own_top, own_total, own_combined = own_parts[kh]
        prev = jnp.where(
            prev_seen, scores_of(queries[kh], head_columns(k_prev, kh)), floor_value
        )
        top = jnp.maximum(own_top, jnp.max(prev, axis=-1, keepdims=True))
        prev_probs = jnp.where(prev_seen, jnp.exp(prev - top), 0.0)
        carry = jnp.exp(own_top - top)
        inverse = 1.0 / (carry * own_total + jnp.sum(prev_probs, axis=-1, keepdims=True))
        joined.append((prev_probs.astype(jnp.bfloat16), carry * own_combined, inverse))

    @pl.when(has_below)
    def _():
        kv_copy(1).wait_recv()

    for kh in range(key_heads):
        prev_probs, own_combined, inverse = joined[kh]
        combined = own_combined + jnp.dot(
            prev_probs, head_columns(v_prev, kh), preferred_element_type=jnp.float32
        )
        result = (combined * inverse).astype(jnp.bfloat16)
        for g in range(group_width):
            attn[me, :, head_span(kh * group_width + g)] = result[g * rows : (g + 1) * rows]

    def parts_of(block):
        return 4 if block in (0, n - 1) else 2

    def attn_copy(slot, block, j, target):
        count = 2 * group_rows // parts_of(block)
        half, at = divmod(j * count, group_rows)
        here = attn.at[block, pl.ds(pl.multiple_of(starts[half] + at, count), count)]
        return remote(
            here,
            here,
            send_sem,
            attn_recv_sem.at[sum(parts_of(b) for b in range(block)) + j],
            {"section": target},
        )

    def wide_of(block):
        return block.astype(jnp.float32)

    def run(s):
        onward = {b: (s + 1 if b < s else s - 1) for b in range(n) if b != s}
        onward = {b: t for b, t in onward.items() if 0 <= t < n}
        squares = []
        started, passed, paired = [], [], []

        spans = [cut(pieces_of(s, b, n)) for b in range(n)]
        bases = [sum(map(len, spans[:b])) for b in range(n)]

        def pair_copy(b, j, c):
            span = spans[b][c]
            at = bases[b] + c if j == 0 else bases[-1] + len(spans[-1]) + b
            return remote(
                pair_send.at[b, j, :, span],
                pair_recv.at[b, j, :, span],
                send_sem,
                pair_recv_sem.at[at],
                {"head": partner},
            )

        def far_copy(b, c):
            span = spans[b][c]
            return remote(
                far_send.at[b, :, span],
                far_recv.at[b, :, span],
                send_sem,
                far_recv_sem.at[bases[b] + c],
                {"head": far},
            )

        def done_copy(b, c):
            span = spans[b][c]
            return remote(
                done_send.at[b, :, span],
                done_recv.at[s, :, span],
                send_sem,
                done_recv_sem.at[s],
                {"section": b},
            )

        def whole(ref, send_sem, recv_sem):
            return remote(ref, ref, send_sem, recv_sem, {"head": partner})


        def wait_kv_sent():
            for i, source in enumerate((k_v, v_v)):
                remote(
                    source, source, kv_send_sem, kv_recv_sem.at[0], {"section": s + 1}
                ).wait_send()

        def send_own(step, j):
            if s == 0 and not started:
                wait_kv_sent()
                pl.semaphore_signal(
                    cleared, inc=1, device_id={"head": partner}, device_id_type=MESH
                )
                pl.semaphore_wait(cleared, 1)
            started.append(parts_of(s))
            attn_copy(0, s, j, s + step).start()

        def relay(b, j):
            attn_copy(1, b, j, s).wait_recv()
            if b in onward:
                passed.append(parts_of(b))
                attn_copy(1, b, j, onward[b]).start()

        def multiply(b, j):
            left = jnp.concatenate(
                [
                    attn[b, pl.ds(pl.multiple_of(starts[j] + side * own_rows, own_rows), own_rows)]
                    for side in (1 - core, core)
                ],
                axis=0,
            )
            for c, span in enumerate(spans[b]):
                product = jnp.dot(left, w_t[:, span], preferred_element_type=jnp.float32)
                pair_send[b, j, :, span] = product[:own_rows].astype(jnp.bfloat16)
                mine[b, j, :, span] = product[own_rows:]
                pair_copy(b, j, c).start()

        def add_pair(b, c):
            span = spans[b][c]
            pair_copy(b, 0, c).wait_recv()
            far_send[b, :, span] = (
                mine[b, 0, :, span] + wide_of(pair_recv[b, 0, :, span])
            ).astype(jnp.bfloat16)
            far_copy(b, c).start()

        def add_far(b, c):
            span = spans[b][c]
            if b not in paired:
                paired.append(b)
                whole(
                    pair_send.at[b, 1], send_sem, pair_recv_sem.at[bases[-1] + len(spans[-1]) + b]
                ).wait_recv()
            far_copy(b, c).wait_recv()
            value = (
                mine[b, 1, :, span]
                + wide_of(pair_recv[b, 1, :, span])
                + wide_of(far_recv[b, :, span])
            ).astype(jnp.bfloat16)
            if b == s:
                done_recv[s, :, span] = value
            else:
                done_send[b, :, span] = value
                done_copy(b, c).start()

        def gather(b, c):
            if b != s:
                whole(done_recv.at[b], send_sem, done_recv_sem.at[b]).wait_recv()
            value = wide_of(done_recv[b])
            squares.append(jnp.sum(value * value, axis=-1, keepdims=True))
            columns = slice(b * width, (b + 1) * width)
            scaled[:, columns] = value * gain_w[:, columns]

        actions = {
            "S": send_own,
            "R": relay,
            "M": multiply,
            "P": add_pair,
            "F": add_far,
            "N": gather,
        }
        for step in ORDERS[n][s]:
            kind, b, j = step[0], int(step[1:-1]), int(step[-1])
            actions[kind](b, j)
        scale = lax.rsqrt(sum(squares) / (n * width) + norm_eps)
        out_ref[...] = (wide_of(res_v[...]) + scaled[...] * scale).astype(out_ref.dtype)

        if s != 0 and s + 1 < n:
            wait_kv_sent()
        for slot, sent in enumerate((started, passed)):
            if sent:
                half = attn.at[0 : round(sum(1 / parts for parts in sent))]
                whole(half, send_sem, attn_recv_sem.at[0]).wait_send()
        whole(pair_send, send_sem, pair_recv_sem.at[0]).wait_send()
        whole(far_send, send_sem, far_recv_sem.at[0]).wait_send()
        whole(done_send.at[: n - 1], send_sem, done_recv_sem.at[s]).wait_send()

    for s in reversed(range(n)):

        @pl.when(me == s)
        def _(s=s):
            run(s)


def fused_local(
    n, heads, queries, token_key_rows, token_value_rows, residual, prefix, out_weight, post_gain
):
    rows = queries.shape[0]
    own_rows = rows // heads
    width = out_weight.shape[1]
    key_heads = token_key_rows.shape[1] // HEAD_SIZE
    low = jnp.bfloat16
    stays = pl.BlockSpec(memory_space=pltpu.HBM)
    vector = pl.BlockSpec(memory_space=pltpu.VMEM)
    dma = pltpu.SemaphoreType.DMA
    weights = out_weight.T
    part = (n, own_rows, width)
    pieces = max(sum(pieces_of(s, b, n) for b in range(n)) for s in range(n))
    return pl.pallas_call(
        functools.partial(fused_kernel, n, heads),
        out_shape=pltpu.VMEM(residual.shape, low),
        in_specs=[stays] * 7,
        out_specs=vector,
        scratch_shapes=[
            pltpu.SMEM(prefix.shape, jnp.int32),
            pltpu.VMEM(queries.shape, low),
            pltpu.VMEM(token_key_rows.shape, low),
            pltpu.VMEM(token_value_rows.shape, low),
            pltpu.VMEM(token_key_rows.shape, low),
            pltpu.VMEM(token_value_rows.shape, low),
            pltpu.VMEM(weights.shape, low),
            pltpu.VMEM(out_weight.shape, low),
            pltpu.VMEM(residual.shape, low),
            pltpu.VMEM(post_gain.shape, jnp.float32),
            pltpu.VMEM((own_rows,) + post_gain.shape, jnp.float32),
            pltpu.VMEM((n, rows, queries.shape[1]), low),
            pltpu.VMEM((n, 2, own_rows, width), low),
            pltpu.VMEM((n, 2, own_rows, width), low),
            pltpu.VMEM((n, 2, own_rows, width), jnp.float32),
            pltpu.VMEM(part, low),
            pltpu.VMEM(part, low),
            pltpu.VMEM(part, low),
            pltpu.VMEM(part, low),
            pltpu.VMEM(residual.shape, jnp.float32),
            dma((3,)),
            dma,
            dma((2,)),
            dma,
            dma((2 * n + 4,)),
            dma((pieces + n,)),
            dma((pieces,)),
            dma((n,)),
            pltpu.SemaphoreType.REGULAR,
        ],
        compiler_params=pltpu.CompilerParams(
            collective_id=0, has_side_effects=True, vmem_limit_bytes=VMEM_LIMIT
        ),
    )(prefix, queries, token_key_rows, token_value_rows, weights, residual, post_gain)


def shifted(value, axis, steps):
    count = lax.axis_size(axis)
    leading, last = (max(0, -steps), min(count, count - steps))
    return lax.ppermute(value, axis, [(source, source + steps) for source in range(leading, last)])


def empty_state(row_count, key_heads, group_width):
    running_max = jnp.full((key_heads, group_width, row_count), floor_value, jnp.float32)
    running_sum = jnp.zeros((key_heads, group_width, row_count), jnp.float32)
    weighted = jnp.zeros((row_count, key_heads, group_width, HEAD_SIZE), jnp.float32)
    return (running_max, running_sum, weighted)


def attend(
    status, query_tile_block, query_pos, lower_pos, key_tile_block, value_tile_block, key_pos
):
    running_max, running_sum, weighted = status
    row_count = query_tile_block.shape[0]
    key_heads = key_tile_block.shape[1] // HEAD_SIZE
    group_width = query_tile_block.shape[1] // (key_heads * HEAD_SIZE)
    query_four = query_tile_block.reshape(row_count, key_heads, group_width, HEAD_SIZE)
    key_three = key_tile_block.reshape(key_tile_block.shape[0], key_heads, HEAD_SIZE)
    value_three = value_tile_block.reshape(value_tile_block.shape[0], key_heads, HEAD_SIZE)
    scores = (
        jnp.einsum("qkgd,pkd->kgqp", query_four, key_three, preferred_element_type=jnp.float32)
        * score_scale
    )
    visible = (key_pos[None, :] <= query_pos[:, None]) & (key_pos[None, :] >= lower_pos)
    masked = jnp.where(visible, scores, floor_value)
    new_max = jnp.maximum(running_max, jnp.max(masked, axis=-1))
    carry_scale = jnp.exp(running_max - new_max)
    weights = jnp.where(visible, jnp.exp(masked - new_max[..., None]), 0.0)
    running_sum = carry_scale * running_sum + jnp.sum(weights, axis=-1)
    product = jnp.einsum(
        "kgqp,pkd->qkgd",
        weights.astype(jnp.bfloat16),
        value_three,
        preferred_element_type=jnp.float32,
    )
    weighted = jnp.transpose(carry_scale, (2, 0, 1))[..., None] * weighted + product
    return (new_max, running_sum, weighted)


def local(queries, token_key_rows, token_value_rows, residual, prefix, out_weight, post_gain):
    row_count = queries.shape[0]
    key_heads = token_key_rows.shape[1] // HEAD_SIZE
    group_width = queries.shape[1] // (key_heads * HEAD_SIZE)
    section_total = lax.axis_size("section")
    section_index = lax.axis_index("section")
    reachable_blocks = 3 * section_total // 8
    base_rows = jnp.arange(row_count, dtype=jnp.int32)
    own_pos = section_index * row_count + base_rows
    seen_tokens = jnp.minimum(section_index * row_count, prefix[section_index])
    lower_pos = section_index * row_count - seen_tokens
    block_count = (seen_tokens + row_count - 1) // row_count
    blank = empty_state(row_count, key_heads, group_width)
    states = attend(blank, queries, own_pos, lower_pos, token_key_rows, token_value_rows, own_pos)

    def process(distance, key_tile_block, value_tile_block, mine):
        key_pos = (section_index - distance) * row_count + base_rows
        use_mine = distance <= block_count
        return lax.cond(
            use_mine,
            lambda current: attend(
                current, queries, own_pos, lower_pos, key_tile_block, value_tile_block, key_pos
            ),
            lambda current: current,
            mine,
        )

    held_keys = token_key_rows[None]
    held_values = token_value_rows[None]
    stride = 1
    while stride <= reachable_blocks:
        amount_moved = min(stride, reachable_blocks + 1 - stride)
        moved_keys, moved_values = shifted(
            (held_keys[:amount_moved], held_values[:amount_moved]), "section", stride
        )
        held_keys = jnp.concatenate([held_keys, moved_keys], axis=0)
        held_values = jnp.concatenate([held_values, moved_values], axis=0)
        stride = stride * 2

    def visit_block(distance, inner):
        key_tile_block = lax.dynamic_index_in_dim(held_keys, distance, 0, keepdims=False)
        value_tile_block = lax.dynamic_index_in_dim(held_values, distance, 0, keepdims=False)
        return process(distance, key_tile_block, value_tile_block, inner)

    states = lax.fori_loop(1, reachable_blocks + 1, visit_block, states)
    attention = states[2] / jnp.transpose(states[1], (2, 0, 1))[..., None]
    attention = attention.reshape(row_count, key_heads * group_width * HEAD_SIZE).astype(
        jnp.bfloat16
    )
    partial_out = jnp.dot(
        attention,
        lax.all_gather(out_weight, "section", axis=1, tiled=True),
        preferred_element_type=jnp.float32,
    )
    summed = lax.psum_scatter(
        partial_out.astype(jnp.bfloat16), "head", scatter_dimension=0, tiled=True
    ).astype(jnp.float32)
    mean_square = jnp.mean(summed * summed, axis=-1, keepdims=True)
    normed = summed * lax.rsqrt(mean_square + norm_eps) * post_gain[None, :]
    return (residual.astype(jnp.float32) + normed).astype(jnp.bfloat16)


def solution(mesh):
    placed = (
        P(("groups", "section"), "head"),
        P(("groups", "section"), "head"),
        P(("groups", "section"), "head"),
        P(("groups", "section", "head"), None),
        P("groups"),
        P("head", "section"),
        P(),
    )
    n, heads = mesh.shape["section"], mesh.shape["head"]
    body = local
    if n in ORDERS and 3 * n // 8 == 1 and heads == 4:
        body = functools.partial(fused_local, n, heads)
    return jax.shard_map(
        body,
        mesh=mesh,
        in_specs=placed,
        out_specs=P(("groups", "section", "head"), None),
        check_vma=False,
    )
```

```python
import functools

import jax
import jax.numpy as jnp
from jax import lax
from jax.experimental import pallas as pl
from jax.experimental.pallas import tpu as pltpu
from jax.sharding import PartitionSpec as P

HEAD_SIZE = 128


score_scale = 168.0 ** (-0.5)
floor_value = -1e30
norm_eps = 1e-06
LANES = 128
FARTHER = 1
VMEM_LIMIT = (60 * 1024 - 720) * 1024
MESH = pl.DeviceIdType.MESH


ORDERS = {
    4: (
        (
            "M00", "M01", "S10", "S11", "S12", "S13", "P00", "R10", "M10", "R11", "P10", "P11",
            "M11", "R20", "M20", "R21", "P20", "P21", "M21", "F10", "F11", "R30", "R31", "M30",
            "P30", "P31", "F20", "R32", "F21", "R33", "M31", "F30", "F31", "F00", "N00", "N10",
            "N20", "N30",
        ),
        (
            "S-10", "S10", "S-11", "S11", "M10", "M11", "P10", "R00", "R01", "M00", "R02", "R03",
            "P00", "P01", "R20", "M20", "R21", "P20", "P21", "M01", "M21", "R30", "R31", "M30",
            "R32", "P30", "P31", "R33", "M31", "F00", "F01", "F20", "F21", "F30", "F31", "F10",
            "N10", "N00", "N20", "N30",
        ),
        (
            "S-10", "S10", "S-11", "S11", "M20", "M21", "P20", "R10", "M10", "R30", "R31", "P10",
            "P11", "R00", "R32", "R01", "M00", "R33", "P00", "P01", "R02", "R03", "R11", "M11",
            "M01", "F10", "F11", "M30", "P30", "P31", "M31", "F00", "F01", "F30", "F31", "F20",
            "N20", "N30", "N10", "N00",
        ),
        (
            "S-10", "S-11", "S-12", "S-13", "M30", "M31", "P30", "R20", "M20", "P20", "P21",
            "R21", "M21", "R00", "R01", "M00", "P00", "P01", "R10", "M10", "F20", "F21", "R02",
            "R03", "M01", "P10", "P11", "F00", "F01", "R11", "M11", "F10", "F11", "F30", "N30",
            "N10", "N00", "N20",
        ),
    ),
}


def pieces_of(s, b, n):
    return 1 if abs(b - s) < FARTHER else 2


def fused_kernel(
    n,
    heads,
    prefix_hbm,
    q_hbm,
    k_hbm,
    v_hbm,
    w_hbm,
    res_hbm,
    gain_hbm,
    out_ref,
    prefix_ref,
    q_v,
    k_v,
    v_v,
    k_prev,
    v_prev,
    w_v,
    w_t,
    res_v,
    gain_v,
    gain_w,
    attn,
    pair_send,
    pair_recv,
    mine,
    far_send,
    far_recv,
    done_send,
    done_recv,
    scaled,
    load_sem,
    kv_send_sem,
    kv_recv_sem,
    send_sem,
    attn_recv_sem,
    pair_recv_sem,
    far_recv_sem,
    done_recv_sem,
    cleared,
):
    me = lax.axis_index("section")
    h = lax.axis_index("head")
    rows = q_hbm.shape[0]
    own_rows = rows // heads
    core = lax.rem(h, 2)
    partner = h + 1 - 2 * core
    far = lax.rem(h + 2, heads)
    group_rows = 2 * own_rows
    starts = [
        pl.multiple_of(lax.rem(h // 2 + 1 + j, 2) * group_rows, group_rows) for j in range(2)
    ]
    key_heads = k_hbm.shape[1] // HEAD_SIZE
    group_width = q_hbm.shape[1] // k_hbm.shape[1]
    width = w_hbm.shape[0]

    def cut(count):
        edges = [LANES * round(width * c / (count * LANES)) for c in range(count)] + [width]
        return [slice(a, b) for a, b in zip(edges, edges[1:])]

    def remote(source, target, send_sem, recv_sem, where):
        return pltpu.make_async_remote_copy(
            src_ref=source,
            dst_ref=target,
            send_sem=send_sem,
            recv_sem=recv_sem,
            device_id=where,
            device_id_type=MESH,
        )

    loads = [
        pltpu.make_async_copy(source, target, load_sem.at[(i + 2) // 3])
        for i, (source, target) in enumerate(
            (
                (prefix_hbm, prefix_ref),
                (q_hbm, q_v),
                (k_hbm, k_v),
                (v_hbm, v_v),
                (w_hbm, w_v),
                (res_hbm, res_v),
                (gain_hbm, gain_v),
            )
        )
    ]
    has_below, has_above = me > 0, me + 1 < n
    barrier = pltpu.get_barrier_semaphore()
    for there, step in ((has_below, -1), (has_above, 1)):

        @pl.when(there)
        def _(step=step):
            pl.semaphore_signal(
                barrier, inc=1, device_id={"section": me + step}, device_id_type=MESH
            )

    for other in (partner, far):
        pl.semaphore_signal(barrier, inc=1, device_id={"head": other}, device_id_type=MESH)
    for load in loads:
        load.start()
    for load in loads[:4]:
        load.wait()
    pl.semaphore_wait(
        barrier, 2 + jnp.where(has_below, 1, 0) + jnp.where(has_above, 1, 0)
    )

    def head_span(at):
        return slice(at * HEAD_SIZE, (at + 1) * HEAD_SIZE)

    def kv_copy(i):
        source, target = ((k_v, k_prev), (v_v, v_prev))[i]
        above = {"section": lax.rem(me + 1, n)}
        return remote(source, target, kv_send_sem, kv_recv_sem.at[i], above)

    @pl.when(has_above)
    def _():
        for i in range(2):
            kv_copy(i).start()

    @pl.when(me == 0)
    def _():
        k_prev[...] = jnp.zeros_like(k_prev)
        v_prev[...] = jnp.zeros_like(v_prev)

    seen = jnp.minimum(me * rows, prefix_ref[me])
    wide = group_width * rows
    q_row = lax.rem(lax.broadcasted_iota(jnp.int32, (wide, rows), 0), rows)
    k_col = lax.broadcasted_iota(jnp.int32, (wide, rows), 1)
    own_seen = k_col <= q_row
    prev_seen = k_col >= rows - seen

    def head_columns(ref, at):
        return ref[:, head_span(at)]

    def scores_of(query, key):
        return (
            lax.dot_general(
                query, key, (((1,), (1,)), ((), ())), preferred_element_type=jnp.float32
            )
            * score_scale
        )

    queries = [
        jnp.concatenate(
            [head_columns(q_v, kh * group_width + g) for g in range(group_width)], axis=0
        )
        for kh in range(key_heads)
    ]
    own_parts = []
    for kh in range(key_heads):
        own = jnp.where(own_seen, scores_of(queries[kh], head_columns(k_v, kh)), floor_value)
        own_top = jnp.max(own, axis=-1, keepdims=True)
        own_probs = jnp.where(own_seen, jnp.exp(own - own_top), 0.0)
        own_total = jnp.sum(own_probs, axis=-1, keepdims=True)
        own_combined = jnp.dot(
            own_probs.astype(jnp.bfloat16),
            head_columns(v_v, kh),
            preferred_element_type=jnp.float32,
        )
        own_parts.append((own_top, own_total, own_combined))

    for load in loads[4:]:
        load.wait()
    w_t[...] = w_v[...].T
    gain_w[...] = jnp.broadcast_to(gain_v[...][None, :], gain_w.shape)

    @pl.when(has_below)
    def _():
        kv_copy(0).wait_recv()

    joined = []
    for kh in range(key_heads):
        own_top, own_total, own_combined = own_parts[kh]
        prev = jnp.where(
            prev_seen, scores_of(queries[kh], head_columns(k_prev, kh)), floor_value
        )
        top = jnp.maximum(own_top, jnp.max(prev, axis=-1, keepdims=True))
        prev_probs = jnp.where(prev_seen, jnp.exp(prev - top), 0.0)
        carry = jnp.exp(own_top - top)
        inverse = 1.0 / (carry * own_total + jnp.sum(prev_probs, axis=-1, keepdims=True))
        joined.append((prev_probs.astype(jnp.bfloat16), carry * own_combined, inverse))

    @pl.when(has_below)
    def _():
        kv_copy(1).wait_recv()

    for kh in range(key_heads):
        prev_probs, own_combined, inverse = joined[kh]
        combined = own_combined + jnp.dot(
            prev_probs, head_columns(v_prev, kh), preferred_element_type=jnp.float32
        )
        result = (combined * inverse).astype(jnp.bfloat16)
        for g in range(group_width):
            attn[me, :, head_span(kh * group_width + g)] = result[g * rows : (g + 1) * rows]

    def parts_of(block):
        return 4 if block in (0, n - 1) else 2

    def attn_copy(slot, block, j, target):
        count = 2 * group_rows // parts_of(block)
        half, at = divmod(j * count, group_rows)
        here = attn.at[block, pl.ds(pl.multiple_of(starts[half] + at, count), count)]
        return remote(
            here,
            here,
            send_sem,
            attn_recv_sem.at[sum(parts_of(b) for b in range(block)) + j],
            {"section": target},
        )

    def wide_of(block):
        return block.astype(jnp.float32)

    def run(s):
        onward = {b: (s + 1 if b < s else s - 1) for b in range(n) if b != s}
        onward = {b: t for b, t in onward.items() if 0 <= t < n}
        squares = []
        started, passed, paired = [], [], []

        spans = [cut(pieces_of(s, b, n)) for b in range(n)]
        bases = [sum(map(len, spans[:b])) for b in range(n)]

        def pair_copy(b, j, c):
            span = spans[b][c]
            at = bases[b] + c if j == 0 else bases[-1] + len(spans[-1]) + b
            return remote(
                pair_send.at[b, j, :, span],
                pair_recv.at[b, j, :, span],
                send_sem,
                pair_recv_sem.at[at],
                {"head": partner},
            )

        def far_copy(b, c):
            span = spans[b][c]
            return remote(
                far_send.at[b, :, span],
                far_recv.at[b, :, span],
                send_sem,
                far_recv_sem.at[bases[b] + c],
                {"head": far},
            )

        def done_copy(b, c):
            span = spans[b][c]
            return remote(
                done_send.at[b, :, span],
                done_recv.at[s, :, span],
                send_sem,
                done_recv_sem.at[s],
                {"section": b},
            )

        def whole(ref, send_sem, recv_sem):
            return remote(ref, ref, send_sem, recv_sem, {"head": partner})


        def wait_kv_sent():
            for i, source in enumerate((k_v, v_v)):
                remote(
                    source, source, kv_send_sem, kv_recv_sem.at[0], {"section": s + 1}
                ).wait_send()

        def send_own(step, j):
            if s == 0 and not started:
                wait_kv_sent()
                pl.semaphore_signal(
                    cleared, inc=1, device_id={"head": partner}, device_id_type=MESH
                )
                pl.semaphore_wait(cleared, 1)
            started.append(parts_of(s))
            attn_copy(0, s, j, s + step).start()

        def relay(b, j):
            attn_copy(1, b, j, s).wait_recv()
            if b in onward:
                passed.append(parts_of(b))
                attn_copy(1, b, j, onward[b]).start()

        def multiply(b, j):
            left = jnp.concatenate(
                [
                    attn[b, pl.ds(pl.multiple_of(starts[j] + side * own_rows, own_rows), own_rows)]
                    for side in (1 - core, core)
                ],
                axis=0,
            )
            for c, span in enumerate(spans[b]):
                product = jnp.dot(left, w_t[:, span], preferred_element_type=jnp.float32)
                pair_send[b, j, :, span] = product[:own_rows].astype(jnp.bfloat16)
                mine[b, j, :, span] = product[own_rows:]
                pair_copy(b, j, c).start()

        def add_pair(b, c):
            span = spans[b][c]
            pair_copy(b, 0, c).wait_recv()
            far_send[b, :, span] = (
                mine[b, 0, :, span] + wide_of(pair_recv[b, 0, :, span])
            ).astype(jnp.bfloat16)
            far_copy(b, c).start()

        def add_far(b, c):
            span = spans[b][c]
            if b not in paired:
                paired.append(b)
                whole(
                    pair_send.at[b, 1], send_sem, pair_recv_sem.at[bases[-1] + len(spans[-1]) + b]
                ).wait_recv()
            far_copy(b, c).wait_recv()
            value = (
                mine[b, 1, :, span]
                + wide_of(pair_recv[b, 1, :, span])
                + wide_of(far_recv[b, :, span])
            ).astype(jnp.bfloat16)
            if b == s:
                done_recv[s, :, span] = value
            else:
                done_send[b, :, span] = value
                done_copy(b, c).start()

        def gather(b, c):
            if b != s:
                whole(done_recv.at[b], send_sem, done_recv_sem.at[b]).wait_recv()
            value = wide_of(done_recv[b])
            squares.append(jnp.sum(value * value, axis=-1, keepdims=True))
            columns = slice(b * width, (b + 1) * width)
            scaled[:, columns] = value * gain_w[:, columns]

        actions = {
            "S": send_own,
            "R": relay,
            "M": multiply,
            "P": add_pair,
            "F": add_far,
            "N": gather,
        }
        for step in ORDERS[n][s]:
            kind, b, j = step[0], int(step[1:-1]), int(step[-1])
            actions[kind](b, j)
        scale = lax.rsqrt(sum(squares) / (n * width) + norm_eps)
        out_ref[...] = (wide_of(res_v[...]) + scaled[...] * scale).astype(out_ref.dtype)

        if s != 0 and s + 1 < n:
            wait_kv_sent()
        for slot, sent in enumerate((started, passed)):
            if sent:
                half = attn.at[0 : round(sum(1 / parts for parts in sent))]
                whole(half, send_sem, attn_recv_sem.at[0]).wait_send()
        whole(pair_send, send_sem, pair_recv_sem.at[0]).wait_send()
        whole(far_send, send_sem, far_recv_sem.at[0]).wait_send()
        whole(done_send.at[: n - 1], send_sem, done_recv_sem.at[s]).wait_send()

    for s in reversed(range(n)):

        @pl.when(me == s)
        def _(s=s):
            run(s)


def fused_local(
    n, heads, queries, token_key_rows, token_value_rows, residual, prefix, out_weight, post_gain
):
    rows = queries.shape[0]
    own_rows = rows // heads
    width = out_weight.shape[1]
    key_heads = token_key_rows.shape[1] // HEAD_SIZE
    low = jnp.bfloat16
    stays = pl.BlockSpec(memory_space=pltpu.HBM)
    vector = pl.BlockSpec(memory_space=pltpu.VMEM)
    dma = pltpu.SemaphoreType.DMA
    weights = out_weight.T
    part = (n, own_rows, width)
    pieces = max(sum(pieces_of(s, b, n) for b in range(n)) for s in range(n))
    return pl.pallas_call(
        functools.partial(fused_kernel, n, heads),
        out_shape=pltpu.VMEM(residual.shape, low),
        in_specs=[stays] * 7,
        out_specs=vector,
        scratch_shapes=[
            pltpu.SMEM(prefix.shape, jnp.int32),
            pltpu.VMEM(queries.shape, low),
            pltpu.VMEM(token_key_rows.shape, low),
            pltpu.VMEM(token_value_rows.shape, low),
            pltpu.VMEM(token_key_rows.shape, low),
            pltpu.VMEM(token_value_rows.shape, low),
            pltpu.VMEM(weights.shape, low),
            pltpu.VMEM(out_weight.shape, low),
            pltpu.VMEM(residual.shape, low),
            pltpu.VMEM(post_gain.shape, jnp.float32),
            pltpu.VMEM((own_rows,) + post_gain.shape, jnp.float32),
            pltpu.VMEM((n, rows, queries.shape[1]), low),
            pltpu.VMEM((n, 2, own_rows, width), low),
            pltpu.VMEM((n, 2, own_rows, width), low),
            pltpu.VMEM((n, 2, own_rows, width), jnp.float32),
            pltpu.VMEM(part, low),
            pltpu.VMEM(part, low),
            pltpu.VMEM(part, low),
            pltpu.VMEM(part, low),
            pltpu.VMEM(residual.shape, jnp.float32),
            dma((3,)),
            dma,
            dma((2,)),
            dma,
            dma((2 * n + 4,)),
            dma((pieces + n,)),
            dma((pieces,)),
            dma((n,)),
            pltpu.SemaphoreType.REGULAR,
        ],
        compiler_params=pltpu.CompilerParams(
            collective_id=0, has_side_effects=True, vmem_limit_bytes=VMEM_LIMIT
        ),
    )(prefix, queries, token_key_rows, token_value_rows, weights, residual, post_gain)


def shifted(value, axis, steps):
    count = lax.axis_size(axis)
    leading, last = (max(0, -steps), min(count, count - steps))
    return lax.ppermute(value, axis, [(source, source + steps) for source in range(leading, last)])


def empty_state(row_count, key_heads, group_width):
    running_max = jnp.full((key_heads, group_width, row_count), floor_value, jnp.float32)
    running_sum = jnp.zeros((key_heads, group_width, row_count), jnp.float32)
    weighted = jnp.zeros((row_count, key_heads, group_width, HEAD_SIZE), jnp.float32)
    return (running_max, running_sum, weighted)


def attend(
    status, query_tile_block, query_pos, lower_pos, key_tile_block, value_tile_block, key_pos
):
    running_max, running_sum, weighted = status
    row_count = query_tile_block.shape[0]
    key_heads = key_tile_block.shape[1] // HEAD_SIZE
    group_width = query_tile_block.shape[1] // (key_heads * HEAD_SIZE)
    query_four = query_tile_block.reshape(row_count, key_heads, group_width, HEAD_SIZE)
    key_three = key_tile_block.reshape(key_tile_block.shape[0], key_heads, HEAD_SIZE)
    value_three = value_tile_block.reshape(value_tile_block.shape[0], key_heads, HEAD_SIZE)
    scores = (
        jnp.einsum("qkgd,pkd->kgqp", query_four, key_three, preferred_element_type=jnp.float32)
        * score_scale
    )
    visible = (key_pos[None, :] <= query_pos[:, None]) & (key_pos[None, :] >= lower_pos)
    masked = jnp.where(visible, scores, floor_value)
    new_max = jnp.maximum(running_max, jnp.max(masked, axis=-1))
    carry_scale = jnp.exp(running_max - new_max)
    weights = jnp.where(visible, jnp.exp(masked - new_max[..., None]), 0.0)
    running_sum = carry_scale * running_sum + jnp.sum(weights, axis=-1)
    product = jnp.einsum(
        "kgqp,pkd->qkgd",
        weights.astype(jnp.bfloat16),
        value_three,
        preferred_element_type=jnp.float32,
    )
    weighted = jnp.transpose(carry_scale, (2, 0, 1))[..., None] * weighted + product
    return (new_max, running_sum, weighted)


def local(queries, token_key_rows, token_value_rows, residual, prefix, out_weight, post_gain):
    row_count = queries.shape[0]
    key_heads = token_key_rows.shape[1] // HEAD_SIZE
    group_width = queries.shape[1] // (key_heads * HEAD_SIZE)
    section_total = lax.axis_size("section")
    section_index = lax.axis_index("section")
    reachable_blocks = 3 * section_total // 8
    base_rows = jnp.arange(row_count, dtype=jnp.int32)
    own_pos = section_index * row_count + base_rows
    seen_tokens = jnp.minimum(section_index * row_count, prefix[section_index])
    lower_pos = section_index * row_count - seen_tokens
    block_count = (seen_tokens + row_count - 1) // row_count
    blank = empty_state(row_count, key_heads, group_width)
    states = attend(blank, queries, own_pos, lower_pos, token_key_rows, token_value_rows, own_pos)

    def process(distance, key_tile_block, value_tile_block, mine):
        key_pos = (section_index - distance) * row_count + base_rows
        use_mine = distance <= block_count
        return lax.cond(
            use_mine,
            lambda current: attend(
                current, queries, own_pos, lower_pos, key_tile_block, value_tile_block, key_pos
            ),
            lambda current: current,
            mine,
        )

    held_keys = token_key_rows[None]
    held_values = token_value_rows[None]
    stride = 1
    while stride <= reachable_blocks:
        amount_moved = min(stride, reachable_blocks + 1 - stride)
        moved_keys, moved_values = shifted(
            (held_keys[:amount_moved], held_values[:amount_moved]), "section", stride
        )
        held_keys = jnp.concatenate([held_keys, moved_keys], axis=0)
        held_values = jnp.concatenate([held_values, moved_values], axis=0)
        stride = stride * 2

    def visit_block(distance, inner):
        key_tile_block = lax.dynamic_index_in_dim(held_keys, distance, 0, keepdims=False)
        value_tile_block = lax.dynamic_index_in_dim(held_values, distance, 0, keepdims=False)
        return process(distance, key_tile_block, value_tile_block, inner)

    states = lax.fori_loop(1, reachable_blocks + 1, visit_block, states)
    attention = states[2] / jnp.transpose(states[1], (2, 0, 1))[..., None]
    attention = attention.reshape(row_count, key_heads * group_width * HEAD_SIZE).astype(
        jnp.bfloat16
    )
    partial_out = jnp.dot(
        attention,
        lax.all_gather(out_weight, "section", axis=1, tiled=True),
        preferred_element_type=jnp.float32,
    )
    summed = lax.psum_scatter(
        partial_out.astype(jnp.bfloat16), "head", scatter_dimension=0, tiled=True
    ).astype(jnp.float32)
    mean_square = jnp.mean(summed * summed, axis=-1, keepdims=True)
    normed = summed * lax.rsqrt(mean_square + norm_eps) * post_gain[None, :]
    return (residual.astype(jnp.float32) + normed).astype(jnp.bfloat16)


def solution(mesh):
    placed = (
        P(("groups", "section"), "head"),
        P(("groups", "section"), "head"),
        P(("groups", "section"), "head"),
        P(("groups", "section", "head"), None),
        P("groups"),
        P("head", "section"),
        P(),
    )
    n, heads = mesh.shape["section"], mesh.shape["head"]
    body = local
    if n in ORDERS and 3 * n // 8 == 1 and heads == 4:
        body = functools.partial(fused_local, n, heads)
    return jax.shard_map(
        body,
        mesh=mesh,
        in_specs=placed,
        out_specs=P(("groups", "section", "head"), None),
        check_vma=False,
    )
```
